32 devices in a mesh: gx: 8 (over z, core), gy: 2 (over y), vert: 2 (over x).
Axes of the slice: x: 2, y: 2, z: 4, core: 2. Of those that a mesh axis runs over, the one named last changes fastest.
Arguments:
- vectors: float32 [16, 64, 16, 128], P('vert', 'gx', 'gy'), may hold values from -6 to 6
- conductivity: float32 [64, 16, 128], P('gx', 'gy'), may hold values from 0.3 to 3
- c_points: int32 [64, 16, 16], P('gx', 'gy'), may hold values from -1 to 127, as said below
Outputs:
- interp: float32 [64, 16, 16, 128], P('gx', 'gy')
- coarse: float32 [64, 16, 9, 256], P('gx', 'gy')
The draws below stay inside these ranges and needn't reach their ends.
Inputs may be any that keep to these rules, and one draw needn't show every extreme that they name: `c_points`: in each tile column the used slots come first, hold distinct positions in increasing order, and number at least 8; some column uses all 16 slots.
All inputs are finite; a program needn't handle non-finite values.
Results may differ from the reference program's by a relative error of at most 0.0003.
Values sent between devices are 32-bit elements; how exact they have to be, the bound alone decides.
A program may use at most 64 MiB of HBM per device.

```python
import math
import jax
import jax.numpy as jnp
from jax import lax

NZ = 128
VECS = 16
CPTS = 16
SWEEPS = 3
NX = 64
NY = 16


def draw_c_points(key, part):
    columns = NX * NY
    keys = jax.random.split(jax.random.fold_in(key, 11), columns)
    chosen = jax.vmap(lambda single: jax.random.permutation(single, NZ)[:CPTS])(keys)
    chosen = jnp.sort(chosen.astype(jnp.int32), axis=1)
    counts = jax.random.randint(jax.random.fold_in(key, 23), (columns,), CPTS // 2, CPTS + 1)
    counts = counts.at[0].set(CPTS)
    slots = jnp.arange(CPTS, dtype=jnp.int32)[None, :]
    result = jnp.where(slots < counts[:, None], chosen, -1)
    return result.reshape(NX, NY, CPTS).astype(jnp.int32)


def level_of(stream_key, dims, pieces, least, largest):
    gain = 1.0
    for dim, parts in pieces:
        heights = jax.random.uniform(jax.random.fold_in(jax.random.fold_in(stream_key, 6), dim), (parts,), jnp.float32, least / len(pieces), largest / len(pieces))
        gain = gain * jnp.repeat(jnp.exp(heights), dims[dim] // parts).reshape((-1,) + (1,) * (len(dims) - 1 - dim))
    return gain


def scatter_about(rng, extent, spread, most, cuts=(), kind=jnp.bfloat16):
    loudness = level_of(rng, extent, cuts, -0.22, 0.18) if cuts else 1.0
    values = jax.random.normal(rng, extent, jnp.float32) * spread * loudness
    return jnp.minimum(jnp.maximum(values, -most), most).astype(kind)


def setup_inputs(seed: int = 0) -> dict:
    streams_of = jax.random.split(jax.random.key(seed), 4)
    return {
        "vectors": scatter_about(streams_of[0], (VECS, NX, NY, NZ), 1.0, 6.0, ((0, 2), (1, 8), (2, 2)), jnp.float32),
        "conductivity": jnp.clip(jnp.exp(math.log(3.0) - 2.3025851 * jax.random.uniform(streams_of[1], (NX, NY, NZ), jnp.float32) ** level_of(streams_of[1], (NX, NY, NZ), ((0, 8), (1, 2)), -0.2, 0.2)), 0.3, 3.0),
        "c_points": draw_c_points(jax.random.fold_in(streams_of[3], 71), 0),
    }


ANISOTROPY = (1.0, 0.6, 0.15)
OMEGA = 0.6
SHIFT = 0.5
RIDGE = 0.1

def stencil_offsets():
    result = []
    for move_x in (-1, 0, 1):
        for move_y in (-1, 0, 1):
            for move_z in (-1, 0, 1):
                if move_x != 0 or move_y != 0 or move_z != 0:
                    result.append((move_x, move_y, move_z))
    return result

def coupling(move):
    weight = 1.0
    for axis_no in range(3):
        if move[axis_no] != 0:
            weight = weight * ANISOTROPY[axis_no]
    return weight

def window_of(move, shape):
    return tuple((slice(1 + move[axis_no], 1 + move[axis_no] + shape[axis_no]) for axis_no in range(3)))

def operator_apply(padded, kpad):
    shape = (kpad.shape[0] - 2, kpad.shape[1] - 2, kpad.shape[2] - 2)
    interior = kpad[1:-1, 1:-1, 1:-1]
    centre = padded[:, 1:-1, 1:-1, 1:-1]
    diagonal = SHIFT * interior * interior
    nearby = jnp.zeros_like(centre)
    for move in stencil_offsets():
        window = window_of(move, shape)
        couple = coupling(move) * interior * kpad[window]
        diagonal = diagonal + couple
        nearby = nearby + couple * padded[(slice(None),) + window]
    return (diagonal * centre - nearby, diagonal, centre)

def jacobi(padded, kpad):
    image, diagonal, centre = operator_apply(padded, kpad)
    alive = diagonal > 0.0
    guarded = jnp.where(alive, diagonal, 1.0)
    return jnp.where(alive, centre - OMEGA * image / guarded, 0.0)

def gram_terms(field, c_points):
    depth = field.shape[-1]
    onehot = (c_points[..., None] == jnp.arange(depth, dtype=jnp.int32)).astype(jnp.float32)
    cvals = jnp.einsum('vxyz,xyjz->vxyj', field, onehot, precision=lax.Precision.HIGHEST)
    right = jnp.einsum('vxyz,vxyj->xyjz', field, cvals, precision=lax.Precision.HIGHEST)
    gram = jnp.einsum('vxyi,vxyj->xyij', cvals, cvals, precision=lax.Precision.HIGHEST)
    return (right, gram, onehot)

def solve_interp(right, gram, onehot):
    slots = gram.shape[-1]
    ridge = RIDGE * jnp.trace(gram, axis1=2, axis2=3) / slots + 1e-06
    system = gram + ridge[:, :, None, None] * jnp.eye(slots, dtype=jnp.float32)
    lower = jnp.linalg.cholesky(system)
    weights = jax.scipy.linalg.cho_solve((lower, True), right)
    c_row = jnp.sum(onehot, axis=2)
    return weights * (1.0 - c_row[:, :, None, :]) + onehot

def galerkin(interp, ppad, kpad):
    shape = (kpad.shape[0] - 2, kpad.shape[1] - 2, kpad.shape[2] - 2)
    interior = kpad[1:-1, 1:-1, 1:-1]
    diagonal = SHIFT * interior * interior
    for move in stencil_offsets():
        diagonal = diagonal + coupling(move) * interior * kpad[window_of(move, shape)]
    blocks = []
    slots = interp.shape[2]
    for move_x in (-1, 0, 1):
        for move_y in (-1, 0, 1):
            if move_x == 0 and move_y == 0:
                image = diagonal[:, :, None, :] * interp
            else:
                image = jnp.zeros_like(interp)
            for move_z in (-1, 0, 1):
                if move_x == 0 and move_y == 0 and (move_z == 0):
                    continue
                move = (move_x, move_y, move_z)
                window = window_of(move, shape)
                couple = coupling(move) * interior * kpad[window]
                source = ppad[window[0], window[1], :, window[2]]
                image = image - couple[:, :, None, :] * source
            block = jnp.einsum('xyiz,xyjz->xyij', interp, image, precision=lax.Precision.HIGHEST)
            blocks.append(block.reshape(shape[0], shape[1], slots * slots))
    return jnp.stack(blocks, axis=2)

def reference(vectors, conductivity, c_points):
    kpad = jnp.pad(conductivity, 1)
    field = vectors
    for turn in range(SWEEPS):
        field = jacobi(jnp.pad(field, ((0, 0), (1, 1), (1, 1), (1, 1))), kpad)
    right, gram, onehot = gram_terms(field, c_points)
    interp = solve_interp(right, gram, onehot)
    ppad = jnp.pad(interp, ((1, 1), (1, 1), (0, 0), (1, 1)))
    coarse = galerkin(interp, ppad, kpad)
    return (interp, coarse)
```

```python
import functools

import jax
import jax.numpy as jnp
from jax import lax
from jax.experimental import pallas as pl
from jax.experimental.pallas import tpu as pltpu
from jax.sharding import PartitionSpec as P

SWEEPS = 3
ANISOTROPY = (1.0, 0.6, 0.15)
OMEGA = 0.6
SHIFT = 0.5
RIDGE = 0.1
HALO = SWEEPS + 1
GROUP = 8
MESH = pl.DeviceIdType.MESH
F32 = jnp.float32
BF16 = jnp.bfloat16


def smear_z(x):
    axis = x.ndim - 1
    depth = x.shape[axis]
    lane = lax.broadcasted_iota(jnp.int32, x.shape, axis)
    below = jnp.where(lane == 0, 0.0, pltpu.roll(x, 1, axis))
    above = jnp.where(lane == depth - 1, 0.0, pltpu.roll(x, depth - 1, axis))
    return x + ANISOTROPY[2] * (below + above)


def smear_xy(ref, row, col, pick):
    return pick(ref, row, col) + ANISOTROPY[0] * (pick(ref, row - 1, col) + pick(ref, row + 1, col))


def smear_row(ref, row, first, last, pick):
    across = {col: smear_xy(ref, row, col, pick) for col in range(first - 1, last + 1)}
    return [
        smear_z(across[col] + ANISOTROPY[1] * (across[col - 1] + across[col + 1]))
        for col in range(first, last)
    ]


def span(move, size):
    if move == 0:
        return pl.ds(0, size), pl.ds(HALO, size)
    if move > 0:
        return pl.ds(size - HALO, HALO), pl.ds(0, HALO)
    return pl.ds(0, HALO), pl.ds(size + HALO, HALO)


def hole(move, size):
    if move == 0:
        return pl.ds(HALO, size)
    return pl.ds(size + HALO, HALO) if move > 0 else pl.ds(0, HALO)


def smooth_kernel(
    nx, ny, nv, v_ref, aux_ref, out_ref, auxe_ref,
    one, two, gain, vsend, vrecv, asend, arecv, fsend, frecv,
):
    size_x, size_y, vecs, depth = v_ref.shape
    wide_x, wide_y = size_x + 2 * HALO, size_y + 2 * HALO
    gx, gy, gv = lax.axis_index("gx"), lax.axis_index("gy"), lax.axis_index("vert")
    moves = [(mx, my) for mx in (-1, 0, 1) for my in (-1, 0, 1) if (mx, my) != (0, 0)]

    def inside(mx, my):
        ok_x = jnp.logical_and(gx + mx >= 0, gx + mx < nx)
        ok_y = jnp.logical_and(gy + my >= 0, gy + my < ny)
        return jnp.logical_and(ok_x, ok_y)

    barrier = pltpu.get_barrier_semaphore()
    total = jnp.int32(nv - 1)
    for mx, my in moves:
        here = inside(mx, my)

        @pl.when(here)
        def _():
            pl.semaphore_signal(
                barrier, inc=1, device_id=(gx + mx, gy + my, gv), device_id_type=MESH
            )

        total = total + here.astype(jnp.int32)
    for step in range(1, nv):
        pl.semaphore_signal(
            barrier, inc=1, device_id=(gx, gy, lax.rem(gv + step, nv)), device_id_type=MESH
        )
    pl.semaphore_wait(barrier, total)

    def copies(no, mx, my):
        from_x, to_x = span(mx, size_x)
        from_y, to_y = span(my, size_y)
        target = (gx + mx, gy + my, gv)
        return (
            pltpu.make_async_remote_copy(
                src_ref=aux_ref.at[from_x, from_y], dst_ref=auxe_ref.at[to_x, to_y],
                send_sem=asend.at[no], recv_sem=arecv.at[no],
                device_id=target, device_id_type=MESH,
            ),
            pltpu.make_async_remote_copy(
                src_ref=v_ref.at[from_x, from_y], dst_ref=one.at[to_x, to_y],
                send_sem=vsend.at[no], recv_sem=vrecv.at[no],
                device_id=target, device_id_type=MESH,
            ),
        )

    def arrivals(no, mx, my):
        other = moves.index((-mx, -my))
        at_x, at_y = hole(mx, size_x), hole(my, size_y)
        target = (gx + mx, gy + my, gv)
        return (
            pltpu.make_async_remote_copy(
                src_ref=auxe_ref.at[at_x, at_y], dst_ref=auxe_ref.at[at_x, at_y],
                send_sem=asend.at[other], recv_sem=arecv.at[other],
                device_id=target, device_id_type=MESH,
            ),
            pltpu.make_async_remote_copy(
                src_ref=one.at[at_x, at_y], dst_ref=one.at[at_x, at_y],
                send_sem=vsend.at[other], recv_sem=vrecv.at[other],
                device_id=target, device_id_type=MESH,
            ),
        )

    for no, (mx, my) in enumerate(moves):

        @pl.when(inside(mx, my))
        def _():
            for copy in copies(no, mx, my):
                copy.start()

        @pl.when(jnp.logical_not(inside(mx, my)))
        def _():
            at_x, at_y = hole(mx, size_x), hole(my, size_y)
            one[at_x, at_y] = jnp.zeros((at_x.size, at_y.size, vecs, depth), F32)
            auxe_ref[at_x, at_y] = jnp.zeros((at_x.size, at_y.size) + aux_ref.shape[2:], F32)

    auxe_ref[pl.ds(HALO, size_x), pl.ds(HALO, size_y)] = aux_ref[...]
    one[pl.ds(HALO, size_x), pl.ds(HALO, size_y)] = v_ref[...]

    for no, (mx, my) in enumerate(moves):

        @pl.when(inside(mx, my))
        def _():
            arrivals(no, mx, my)[0].wait_recv()

    def pick_k(ref, row, col):
        return ref[row, col, 0:1, :]

    def pick_u(ref, row, col):
        return ref[row, col]

    def gains(row, carry):
        around = smear_row(auxe_ref, row, 1, wide_y - 1, pick_k)
        for col in range(1, wide_y - 1):
            mid = pick_k(auxe_ref, row, col)
            below = around[col - 1] - (1.0 - SHIFT) * mid
            alive = mid > 0.0
            value = jnp.where(alive, OMEGA * mid / jnp.where(alive, below, 1.0), 0.0)
            gain[row, col] = jnp.broadcast_to(value, (vecs, depth))
        return carry

    lax.fori_loop(1, wide_x - 1, gains, 0)

    for no, (mx, my) in enumerate(moves):

        @pl.when(inside(mx, my))
        def _():
            arrivals(no, mx, my)[1].wait_recv()

    def scale(row, carry):
        for col in range(wide_y):
            one[row, col] = one[row, col] * jnp.broadcast_to(pick_k(auxe_ref, row, col), (vecs, depth))
        return carry

    lax.fori_loop(0, wide_x, scale, 0)

    def relaxed(ref, row, first, last):
        around = smear_row(ref, row, first, last, pick_u)
        result = []
        for col in range(first, last):
            factor = gain[row, col]
            result.append((1.0 - OMEGA - factor) * ref[row, col] + factor * around[col - first])
        return result

    source, target = one, two
    for sweep in range(1, SWEEPS):

        def step(row, carry, source=source, target=target, sweep=sweep):
            for no, value in enumerate(relaxed(source, row, sweep, wide_y - sweep)):
                target[row, sweep + no] = value
            return carry

        lax.fori_loop(sweep, wide_x - sweep, step, 0)
        source, target = target, source

    def field_copy(row, step):
        return pltpu.make_async_remote_copy(
            src_ref=out_ref.at[gv, row], dst_ref=out_ref.at[gv, row],
            send_sem=fsend.at[step - 1, row], recv_sem=frecv.at[step - 1, row],
            device_id=(gx, gy, lax.rem(gv + step, nv)), device_id_type=MESH,
        )

    rows = size_x + 2

    def last_sweep(row, carry):
        for no, value in enumerate(relaxed(source, row + SWEEPS, SWEEPS, wide_y - SWEEPS)):
            out_ref[gv, row, no] = value

        @pl.when(row >= 1)
        def _():
            for step in range(1, nv):
                field_copy(row - 1, step).start()

        return carry

    lax.fori_loop(0, rows, last_sweep, 0)
    for step in range(1, nv):
        field_copy(rows - 1, step).start()

    for no, (mx, my) in enumerate(moves):

        @pl.when(inside(mx, my))
        def _():
            for copy in copies(no, mx, my):
                copy.wait_send()

    for step in range(1, nv):
        origin = lax.rem(gv - step + nv, nv)
        for row in range(rows):
            field_copy(row, step).wait_send()
            pltpu.make_async_remote_copy(
                src_ref=out_ref.at[origin, row], dst_ref=out_ref.at[origin, row],
                send_sem=fsend.at[step - 1, row], recv_sem=frecv.at[step - 1, row],
                device_id=(gx, gy, origin), device_id_type=MESH,
            ).wait_recv()


def split(x):
    high = x.astype(BF16)
    return high, (x - high.astype(F32)).astype(BF16)


NT = (((1,), (1,)), ((), ()))
NN = (((1,), (0,)), ((), ()))


def dot(a, b, dims):
    return lax.dot_general(a, b, dims, preferred_element_type=F32)


def dot3(a, b, dims):
    return dot(a[0], b[0], dims) + dot(a[0], b[1], dims) + dot(a[1], b[0], dims)


def coarse_kernel(
    size_x, size_y, slots, f_ref, k_ref, c_ref, interp_ref, coarse_ref,
    hot, right_s, gram_s, lh, ll, rh, rl, ch, cl,
):
    nv, cols, vecs, depth = f_ref.shape
    wide_y = size_y + 2
    rows = GROUP * slots
    members = GROUP * nv * vecs
    count = gram_s.shape[0]
    band = size_y * slots

    def lanes(shape):
        return lax.broadcasted_iota(jnp.int32, shape, len(shape) - 1)

    def subs(shape):
        return lax.broadcasted_iota(jnp.int32, shape, len(shape) - 2)

    same = subs((rows, members)) // slots == lanes((rows, members)) // (nv * vecs)
    same_slots = subs((rows, rows)) // slots == lanes((rows, rows)) // slots
    own_lane = subs((rows, depth)) % slots == lanes((rows, depth))
    ones = jnp.ones((depth, depth), BF16)

    def start_of(no):
        return jnp.minimum(no * GROUP, cols - GROUP)

    def gather(no, carry):
        start = start_of(no)
        knots = k_ref[pl.ds(start, GROUP)]
        alive = knots > 0.0
        inverse = jnp.where(alive, 1.0 / jnp.where(alive, knots, 1.0), 0.0)
        field = jnp.concatenate(
            [f_ref[half, pl.ds(start, GROUP)] * inverse for half in range(nv)], axis=1
        ).reshape(members, depth)
        spots = jnp.broadcast_to(
            c_ref[pl.ds(start, GROUP)], (GROUP, slots, depth)
        ).reshape(rows, depth)
        spread = dot(jnp.where(own_lane, spots, 0.0).astype(BF16), ones, NN)
        onehot = jnp.where(spread == lanes((rows, depth)).astype(F32), 1.0, 0.0)
        hot[no] = onehot
        fh, fl = split(field)
        picked = onehot.astype(BF16)
        cvals = jnp.where(same, dot(picked, fh, NT) + dot(picked, fl, NT), 0.0)
        pair = split(cvals)
        right_s[no] = dot3(pair, (fh, fl), NN)
        gram = dot3(pair, pair, NT)
        gram_s[no] = jnp.sum(gram.reshape(GROUP, slots, rows), axis=0)
        return carry

    lax.fori_loop(0, count, gather, 0)

    shape = (count, slots, rows)
    lane = lanes(shape) % slots
    sub = subs(shape)
    system = gram_s[...]
    diagonal = jnp.sum(jnp.where(lane == sub, system, 0.0), axis=1)
    block = jnp.where(same_slots, 1.0, 0.0).astype(BF16)
    first = diagonal.astype(BF16)
    rest = diagonal - first.astype(F32)
    second = rest.astype(BF16)
    third = (rest - second.astype(F32)).astype(BF16)
    trace = dot(first, block, NN) + dot(second, block, NN) + dot(third, block, NN)
    ridge = RIDGE * trace / slots + 1e-06
    system = system + jnp.where(lane == sub, ridge[:, None, :], 0.0)
    flat = (count * slots, rows)
    base = lanes(flat) // slots * slots
    for pivot in range(slots):
        column = jnp.take_along_axis(
            system.reshape(flat), base + pivot, axis=1, mode="promise_in_bounds"
        ).reshape(shape)
        line = system[:, pivot : pivot + 1, :]
        here = lane[:, 0:1, :] == pivot
        line = jnp.where(here, 1.0, line) / column[:, pivot : pivot + 1, :]
        system = jnp.where(
            sub == pivot, line, jnp.where(lane == pivot, 0.0, system) - column * line
        )
    gram_s[...] = system

    def weigh(no, carry):
        start = start_of(no)
        inverse = jnp.where(
            same_slots,
            jnp.broadcast_to(gram_s[no][None], (GROUP, slots, rows)).reshape(rows, rows),
            0.0,
        )
        weights = dot3(split(inverse), split(right_s[no]), NN).reshape(GROUP, slots, depth)
        onehot = hot[no].reshape(GROUP, slots, depth)
        crow = jnp.sum(onehot, axis=1, keepdims=True)
        value = weights * (1.0 - crow) + onehot
        hot_cols = pl.ds(start, GROUP)
        ch[hot_cols] = value
        left = value * k_ref[hot_cols]
        high, low = split(left.reshape(rows, depth))
        lh[hot_cols] = high.reshape(GROUP, slots, depth)
        ll[hot_cols] = low.reshape(GROUP, slots, depth)
        high, low = split(smear_z(left.reshape(rows, depth)))
        rh[hot_cols] = high.reshape(GROUP, slots, depth)
        rl[hot_cols] = low.reshape(GROUP, slots, depth)
        return carry

    lax.fori_loop(0, count, weigh, 0)

    half = GROUP * slots
    groups = slots * slots // half
    sub_rows = slots // groups
    chosen = subs((sub_rows, half)) == lanes((sub_rows, half)) // slots

    def galerkin(row, carry):
        at = (row + 1) * wide_y
        mine = pl.ds(at + 1, size_y)
        own = ch[mine]
        interp_ref[row] = own
        across = k_ref[pl.ds(at, wide_y)] + ANISOTROPY[0] * (
            k_ref[pl.ds(at - wide_y, wide_y)] + k_ref[pl.ds(at + wide_y, wide_y)]
        )
        along = across[1 : size_y + 1] + ANISOTROPY[1] * (across[0:size_y] + across[2:])
        whole = smear_z(along.reshape(size_y, depth)).reshape(size_y, 1, depth)
        centre = own * (whole + SHIFT * k_ref[mine])
        left = (lh[mine].reshape(band, depth), ll[mine].reshape(band, depth))
        middle = dot3(left, split(centre.reshape(band, depth)), NT)
        for move_x in (-1, 0, 1):
            there = pl.ds(at + move_x * wide_y, wide_y)
            other = (
                rh[there].reshape(wide_y * slots, depth),
                rl[there].reshape(wide_y * slots, depth),
            )
            product = dot3(left, other, NT)
            for col in range(size_y):
                rows_here = slice(col * slots, (col + 1) * slots)
                for move_y in (-1, 0, 1):
                    weight = 1.0
                    if move_x != 0:
                        weight = weight * ANISOTROPY[0]
                    if move_y != 0:
                        weight = weight * ANISOTROPY[1]
                    begin = (col + 1 + move_y) * slots
                    tile = -weight * product[rows_here, begin : begin + slots]
                    if move_x == 0 and move_y == 0:
                        tile = tile + middle[rows_here, col * slots : (col + 1) * slots]
                    spread = jnp.concatenate([tile] * GROUP, axis=1)
                    parts = [
                        jnp.sum(
                            jnp.where(chosen, spread[g * sub_rows : (g + 1) * sub_rows], 0.0),
                            axis=0, keepdims=True,
                        )
                        for g in range(groups)
                    ]
                    order = 3 * (move_x + 1) + move_y + 1
                    coarse_ref[row, col, order : order + 1, :] = jnp.concatenate(parts, axis=1)
        return carry

    lax.fori_loop(0, size_x, galerkin, 0)


def body(nx, ny, nv, vectors, conductivity, c_points):
    vecs, size_x, size_y, depth = vectors.shape
    slots = c_points.shape[-1]
    turned = jnp.transpose(vectors, (1, 2, 0, 3))
    spots = jnp.pad(c_points.astype(F32), ((0, 0), (0, 0), (0, depth - slots)))
    aux = jnp.stack([conductivity, spots], axis=2)
    wide_x, wide_y = size_x + 2 * HALO, size_y + 2 * HALO
    vmem = pl.BlockSpec(memory_space=pltpu.VMEM)
    dma = pltpu.SemaphoreType.DMA
    field, auxe = pl.pallas_call(
        functools.partial(smooth_kernel, nx, ny, nv),
        out_shape=(
            jax.ShapeDtypeStruct((nv, size_x + 2, size_y + 2, vecs, depth), F32),
            jax.ShapeDtypeStruct((wide_x, wide_y, 2, depth), F32),
        ),
        in_specs=[vmem] * 2,
        out_specs=(vmem, vmem),
        scratch_shapes=[
            pltpu.VMEM((wide_x, wide_y, vecs, depth), F32),
            pltpu.VMEM((wide_x, wide_y, vecs, depth), F32),
            pltpu.VMEM((wide_x, wide_y, vecs, depth), F32),
            dma((8,)), dma((8,)), dma((8,)), dma((8,)),
            dma((nv, size_x + 2)), dma((nv, size_x + 2)),
        ],
        compiler_params=pltpu.CompilerParams(collective_id=0, has_side_effects=True),
        name="smooth",
    )(turned, aux)
    cols = (size_x + 2) * (size_y + 2)
    count = -(-cols // GROUP)
    rim = HALO - 1
    near = auxe[rim : wide_x - rim, rim : wide_y - rim].reshape(cols, 2, depth)
    rows = GROUP * slots
    return pl.pallas_call(
        functools.partial(coarse_kernel, size_x, size_y, slots),
        out_shape=(
            jax.ShapeDtypeStruct((size_x, size_y, slots, depth), F32),
            jax.ShapeDtypeStruct((size_x, size_y, 9, slots * slots), F32),
        ),
        in_specs=[vmem] * 3,
        out_specs=(vmem, vmem),
        scratch_shapes=[
            pltpu.VMEM((count, rows, depth), F32),
            pltpu.VMEM((count, rows, depth), F32),
            pltpu.VMEM((count, slots, rows), F32),
            pltpu.VMEM((cols, slots, depth), BF16),
            pltpu.VMEM((cols, slots, depth), BF16),
            pltpu.VMEM((cols, slots, depth), BF16),
            pltpu.VMEM((cols, slots, depth), BF16),
            pltpu.VMEM((cols, slots, depth), F32),
            pltpu.VMEM((8, 128), F32),
        ],
        name="coarse",
    )(field.reshape(nv, cols, vecs, depth), near[:, 0:1], near[:, 1:2])


def solution(mesh):
    placed = (P("vert", "gx", "gy", None), P("gx", "gy", None), P("gx", "gy", None))
    return jax.shard_map(
        functools.partial(body, mesh.shape["gx"], mesh.shape["gy"], mesh.shape["vert"]),
        mesh=mesh,
        in_specs=placed,
        out_specs=(P("gx", "gy", None, None), P("gx", "gy", None, None)),
        check_vma=False,
    )
```

```python
import functools

import jax
import jax.numpy as jnp
from jax import lax
from jax.experimental import pallas as pl
from jax.experimental.pallas import tpu as pltpu
from jax.sharding import PartitionSpec as P

SWEEPS = 3
ANISOTROPY = (1.0, 0.6, 0.15)
OMEGA = 0.6
SHIFT = 0.5
RIDGE = 0.1
HALO = SWEEPS + 1
GROUP = 8
UNROLL = True
MESH = pl.DeviceIdType.MESH
F32 = jnp.float32
BF16 = jnp.bfloat16


def smear_z(x):
    axis = x.ndim - 1
    depth = x.shape[axis]
    lane = lax.broadcasted_iota(jnp.int32, x.shape, axis)
    below = jnp.where(lane == 0, 0.0, pltpu.roll(x, 1, axis))
    above = jnp.where(lane == depth - 1, 0.0, pltpu.roll(x, depth - 1, axis))
    return x + ANISOTROPY[2] * (below + above)


def smear_xy(ref, row, col, pick):
    return pick(ref, row, col) + ANISOTROPY[0] * (pick(ref, row - 1, col) + pick(ref, row + 1, col))


def smear_row(ref, row, first, last, pick):
    across = {col: smear_xy(ref, row, col, pick) for col in range(first - 1, last + 1)}
    return [
        smear_z(across[col] + ANISOTROPY[1] * (across[col - 1] + across[col + 1]))
        for col in range(first, last)
    ]


def span(move, size):
    if move == 0:
        return pl.ds(0, size), pl.ds(HALO, size)
    if move > 0:
        return pl.ds(size - HALO, HALO), pl.ds(0, HALO)
    return pl.ds(0, HALO), pl.ds(size + HALO, HALO)


def hole(move, size):
    if move == 0:
        return pl.ds(HALO, size)
    return pl.ds(size + HALO, HALO) if move > 0 else pl.ds(0, HALO)


def smooth_kernel(
    nx, ny, nv, v_ref, k_ref, c_ref, out_ref, knots_ref, spots_ref,
    one, two, gain, wide_k, wide_c, ksend, krecv, csend, crecv, vsend, vrecv, fsend, frecv,
):
    size_x, size_y, vecs, depth = v_ref.shape
    wide_x, wide_y = size_x + 2 * HALO, size_y + 2 * HALO
    gx, gy, gv = lax.axis_index("gx"), lax.axis_index("gy"), lax.axis_index("vert")
    moves = [(mx, my) for mx in (-1, 0, 1) for my in (-1, 0, 1) if (mx, my) != (0, 0)]

    def inside(mx, my):
        ok_x = jnp.logical_and(gx + mx >= 0, gx + mx < nx)
        ok_y = jnp.logical_and(gy + my >= 0, gy + my < ny)
        return jnp.logical_and(ok_x, ok_y)

    barrier = pltpu.get_barrier_semaphore()
    total = jnp.int32(nv - 1)
    for mx, my in moves:
        here = inside(mx, my)

        @pl.when(here)
        def _():
            pl.semaphore_signal(
                barrier, inc=1, device_id=(gx + mx, gy + my, gv), device_id_type=MESH
            )

        total = total + here.astype(jnp.int32)
    for step in range(1, nv):
        pl.semaphore_signal(
            barrier, inc=1, device_id=(gx, gy, lax.rem(gv + step, nv)), device_id_type=MESH
        )
    pl.semaphore_wait(barrier, total)

    kinds = (
        (k_ref, wide_k, ksend, krecv), (v_ref, one, vsend, vrecv), (c_ref, wide_c, csend, crecv),
    )

    def departure(kind, no):
        mx, my = moves[no]
        source, target, send, recv = kinds[kind]
        from_x, to_x = span(mx, size_x)
        from_y, to_y = span(my, size_y)
        return pltpu.make_async_remote_copy(
            src_ref=source.at[from_x, from_y], dst_ref=target.at[to_x, to_y],
            send_sem=send.at[no], recv_sem=recv.at[no],
            device_id=(gx + mx, gy + my, gv), device_id_type=MESH,
        )

    def arrival(kind, no):
        mx, my = moves[no]
        other = moves.index((-mx, -my))
        _, target, send, recv = kinds[kind]
        place = target.at[hole(mx, size_x), hole(my, size_y)]
        return pltpu.make_async_remote_copy(
            src_ref=place, dst_ref=place, send_sem=send.at[other], recv_sem=recv.at[other],
            device_id=(gx + mx, gy + my, gv), device_id_type=MESH,
        )

    for no, (mx, my) in enumerate(moves):

        @pl.when(inside(mx, my))
        def _():
            for kind in range(3):
                departure(kind, no).start()

        @pl.when(jnp.logical_not(inside(mx, my)))
        def _():
            at_x, at_y = hole(mx, size_x), hole(my, size_y)
            for source, target, _, _ in kinds:
                target[at_x, at_y] = jnp.zeros(
                    (at_x.size, at_y.size) + source.shape[2:], source.dtype
                )

    for source, target, _, _ in kinds:
        target[pl.ds(HALO, size_x), pl.ds(HALO, size_y)] = source[...]

    for no, (mx, my) in enumerate(moves):

        @pl.when(inside(mx, my))
        def _():
            arrival(0, no).wait_recv()

    def pick_k(ref, row, col):
        return ref[row, col, 0:1, :]

    def pick_u(ref, row, col):
        return ref[row, col]

    def gains(row, carry):
        around = smear_row(wide_k, row, 1, wide_y - 1, pick_k)
        for col in range(1, wide_y - 1):
            mid = pick_k(wide_k, row, col)
            below = around[col - 1] - (1.0 - SHIFT) * mid
            alive = mid > 0.0
            value = jnp.where(alive, OMEGA * mid / jnp.where(alive, below, 1.0), 0.0)
            gain[row, col] = jnp.broadcast_to(value, (vecs, depth))
        return carry

    lax.fori_loop(1, wide_x - 1, gains, 0)

    for no, (mx, my) in enumerate(moves):

        @pl.when(inside(mx, my))
        def _():
            arrival(1, no).wait_recv()
            arrival(2, no).wait_recv()

    def scale(row, carry):
        for col in range(wide_y):
            one[row, col] = one[row, col] * jnp.broadcast_to(pick_k(wide_k, row, col), (vecs, depth))
        return carry

    lax.fori_loop(0, wide_x, scale, 0)

    def relaxed(ref, row, first, last):
        around = smear_row(ref, row, first, last, pick_u)
        result = []
        for col in range(first, last):
            factor = gain[row, col]
            result.append((1.0 - OMEGA - factor) * ref[row, col] + factor * around[col - first])
        return result

    source, target = one, two
    for sweep in range(1, SWEEPS):

        def step(row, carry, source=source, target=target, sweep=sweep):
            for no, value in enumerate(relaxed(source, row, sweep, wide_y - sweep)):
                target[row, sweep + no] = value
            return carry

        lax.fori_loop(sweep, wide_x - sweep, step, 0)
        source, target = target, source

    def field_copy(row, step):
        return pltpu.make_async_remote_copy(
            src_ref=out_ref.at[gv, row], dst_ref=out_ref.at[gv, row],
            send_sem=fsend.at[step - 1, row], recv_sem=frecv.at[step - 1, row],
            device_id=(gx, gy, lax.rem(gv + step, nv)), device_id_type=MESH,
        )

    rows = size_x + 2

    def last_sweep(row, carry):
        for no, value in enumerate(relaxed(source, row + SWEEPS, SWEEPS, wide_y - SWEEPS)):
            out_ref[gv, row, no] = value

        @pl.when(row >= 1)
        def _():
            for step in range(1, nv):
                field_copy(row - 1, step).start()

        return carry

    lax.fori_loop(0, rows, last_sweep, 0)
    for step in range(1, nv):
        field_copy(rows - 1, step).start()

    rim_x, rim_y = pl.ds(HALO - 1, size_x + 2), pl.ds(HALO - 1, size_y + 2)
    knots_ref[...] = wide_k[rim_x, rim_y]
    spots_ref[...] = wide_c[rim_x, rim_y]

    for no, (mx, my) in enumerate(moves):

        @pl.when(inside(mx, my))
        def _():
            for kind in range(3):
                departure(kind, no).wait_send()

    for step in range(1, nv):
        origin = lax.rem(gv - step + nv, nv)
        for row in range(rows):
            field_copy(row, step).wait_send()
            pltpu.make_async_remote_copy(
                src_ref=out_ref.at[origin, row], dst_ref=out_ref.at[origin, row],
                send_sem=fsend.at[step - 1, row], recv_sem=frecv.at[step - 1, row],
                device_id=(gx, gy, origin), device_id_type=MESH,
            ).wait_recv()


def split(x):
    high = x.astype(BF16)
    return high, (x - high.astype(F32)).astype(BF16)


NT = (((1,), (1,)), ((), ()))
NN = (((1,), (0,)), ((), ()))


def dot(a, b, dims):
    return lax.dot_general(a, b, dims, preferred_element_type=F32)


def dot3(a, b, dims):
    return dot(a[0], b[0], dims) + dot(a[0], b[1], dims) + dot(a[1], b[0], dims)


def coarse_kernel(
    size_x, size_y, slots, f_ref, k_ref, c_ref, interp_ref, coarse_ref,
    hot, right_s, gram_s, lh, ll, rh, rl, ch,
):
    nv, cols, vecs, depth = f_ref.shape
    wide_y = size_y + 2
    rows = GROUP * slots
    members = GROUP * nv * vecs
    count = gram_s.shape[0]
    padded = -(-wide_y // GROUP) * GROUP
    band = size_y * slots

    def lanes(shape):
        return lax.broadcasted_iota(jnp.int32, shape, len(shape) - 1)

    def subs(shape):
        return lax.broadcasted_iota(jnp.int32, shape, len(shape) - 2)

    same = subs((rows, members)) // slots == lanes((rows, members)) // (nv * vecs)
    same_slots = subs((rows, rows)) // slots == lanes((rows, rows)) // slots
    own_lane = subs((rows, slots)) % slots == lanes((rows, slots))
    ones = jnp.ones((slots, depth), BF16)

    def start_of(no):
        return jnp.minimum(no * GROUP, cols - GROUP)

    def gather(no, carry):
        start = start_of(no)
        knots = k_ref[pl.ds(start, GROUP)]
        alive = knots > 0.0
        inverse = jnp.where(alive, 1.0 / jnp.where(alive, knots, 1.0), 0.0)
        field = jnp.concatenate(
            [f_ref[half, pl.ds(start, GROUP)] * inverse for half in range(nv)], axis=1
        ).reshape(members, depth)
        spots = jnp.broadcast_to(
            c_ref[pl.ds(start, GROUP)].astype(F32), (GROUP, slots, slots)
        ).reshape(rows, slots)
        spread = dot(jnp.where(own_lane, spots, 0.0).astype(BF16), ones, NN)
        onehot = jnp.where(spread == lanes((rows, depth)).astype(F32), 1.0, 0.0)
        hot[no] = onehot
        fh, fl = split(field)
        picked = onehot.astype(BF16)
        cvals = jnp.where(same, dot(picked, fh, NT) + dot(picked, fl, NT), 0.0)
        pair = split(cvals)
        right_s[no] = dot3(pair, (fh, fl), NN)
        gram = dot3(pair, pair, NT)
        gram_s[no] = jnp.sum(gram.reshape(GROUP, slots, rows), axis=0)
        return carry

    lax.fori_loop(0, count, gather, 0, unroll=UNROLL)

    shape = (count, slots, rows)
    lane = lanes(shape) % slots
    sub = subs(shape)
    system = gram_s[...]
    diagonal = jnp.sum(jnp.where(lane == sub, system, 0.0), axis=1)
    block = jnp.where(same_slots, 1.0, 0.0).astype(BF16)
    first = diagonal.astype(BF16)
    rest = diagonal - first.astype(F32)
    second = rest.astype(BF16)
    third = (rest - second.astype(F32)).astype(BF16)
    trace = dot(first, block, NN) + dot(second, block, NN) + dot(third, block, NN)
    ridge = RIDGE * trace / slots + 1e-06
    system = system + jnp.where(lane == sub, ridge[:, None, :], 0.0)
    flat = (count * slots, rows)
    base = lanes(flat) // slots * slots
    for pivot in range(slots):
        column = jnp.take_along_axis(
            system.reshape(flat), base + pivot, axis=1, mode="promise_in_bounds"
        ).reshape(shape)
        line = system[:, pivot : pivot + 1, :]
        here = lane[:, 0:1, :] == pivot
        line = jnp.where(here, 1.0, line) / column[:, pivot : pivot + 1, :]
        system = jnp.where(
            sub == pivot, line, jnp.where(lane == pivot, 0.0, system) - column * line
        )
    gram_s[...] = system

    def weigh(no, carry):
        start = start_of(no)
        inverse = jnp.where(
            same_slots,
            jnp.broadcast_to(gram_s[no][None], (GROUP, slots, rows)).reshape(rows, rows),
            0.0,
        )
        weights = dot3(split(inverse), split(right_s[no]), NN).reshape(GROUP, slots, depth)
        onehot = hot[no].reshape(GROUP, slots, depth)
        crow = jnp.sum(onehot, axis=1, keepdims=True)
        value = weights * (1.0 - crow) + onehot
        hot_cols = pl.ds(start, GROUP)
        ch[hot_cols] = value
        left = value * k_ref[hot_cols]
        high, low = split(left.reshape(rows, depth))
        lh[hot_cols] = high.reshape(GROUP, slots, depth)
        ll[hot_cols] = low.reshape(GROUP, slots, depth)
        high, low = split(smear_z(left.reshape(rows, depth)))
        rh[hot_cols] = high.reshape(GROUP, slots, depth)
        rl[hot_cols] = low.reshape(GROUP, slots, depth)
        return carry

    lax.fori_loop(0, count, weigh, 0, unroll=UNROLL)

    half = GROUP * slots
    groups = slots * slots // half
    tall = (GROUP, half)
    pick_row = lanes(tall) // slots
    out_row = subs(tall)

    def merge(tiles):
        hop = GROUP // 2
        while hop >= 1:
            up = out_row // hop % 2 == 1
            straight = up == (pick_row // hop % 2 == 1)
            merged = []
            for no in range(hop):
                one, two = tiles[no], tiles[no + hop]
                same_place = jnp.where(up, two, one)
                moved = jnp.where(up, one, two)
                down = pltpu.roll(moved, hop, 0)
                if 2 * hop != GROUP:
                    down = jnp.where(up, down, pltpu.roll(moved, GROUP - hop, 0))
                merged.append(jnp.where(straight, same_place, down))
            tiles = merged
            hop //= 2
        return tiles[0]

    block_lane = lanes((slots, half)) % slots

    def galerkin(row, carry):
        at = (row + 1) * wide_y
        mine = pl.ds(at + 1, size_y)
        own = ch[mine]
        interp_ref[row] = own
        across = k_ref[pl.ds(at, wide_y)] + ANISOTROPY[0] * (
            k_ref[pl.ds(at - wide_y, wide_y)] + k_ref[pl.ds(at + wide_y, wide_y)]
        )
        along = across[1 : size_y + 1] + ANISOTROPY[1] * (across[0:size_y] + across[2:])
        whole = smear_z(along.reshape(size_y, depth)).reshape(size_y, 1, depth)
        left = (lh[mine].reshape(band, depth), ll[mine].reshape(band, depth))
        right = rh[mine].astype(F32) + rl[mine].astype(F32)
        centre = right - own * (whole + SHIFT * k_ref[mine])
        middle = dot3(left, split(centre.reshape(band, depth)), NT)
        for move_x in (-1, 0, 1):
            there = pl.ds(at + move_x * wide_y, padded)
            other = (
                rh[there].reshape(padded * slots, depth),
                rl[there].reshape(padded * slots, depth),
            )
            product = dot3(left, other, NT)
            for move_y in (-1, 0, 1):
                weight = 1.0
                if move_x != 0:
                    weight = weight * ANISOTROPY[0]
                if move_y != 0:
                    weight = weight * ANISOTROPY[1]
                order = 3 * (move_x + 1) + move_y + 1
                for chunk in range(0, size_y, GROUP):
                    spread = []
                    for col in range(chunk, chunk + GROUP):
                        central = move_x == 0 and move_y == 0
                        origin = middle if central else product
                        place = col if central else col + 1 + move_y
                        first_lane = place // GROUP * half
                        values = origin[
                            col * slots : (col + 1) * slots, first_lane : first_lane + half
                        ]
                        spread.append(
                            jnp.take_along_axis(
                                values, block_lane + place % GROUP * slots, axis=1,
                                mode="promise_in_bounds",
                            )
                        )
                    parts = [
                        merge([tile[g * GROUP : (g + 1) * GROUP] for tile in spread])
                        for g in range(groups)
                    ]
                    coarse_ref[row, order, chunk : chunk + GROUP, :] = -weight * jnp.concatenate(
                        parts, axis=1
                    )
        return carry

    lax.fori_loop(0, size_x, galerkin, 0)


def body(nx, ny, nv, vectors, conductivity, c_points):
    vecs, size_x, size_y, depth = vectors.shape
    slots = c_points.shape[-1]
    turned = jnp.transpose(vectors, (1, 2, 0, 3))
    wide_x, wide_y = size_x + 2 * HALO, size_y + 2 * HALO
    cols = (size_x + 2) * (size_y + 2)
    vmem = pl.BlockSpec(memory_space=pltpu.VMEM)
    dma = pltpu.SemaphoreType.DMA
    field, knots, spots = pl.pallas_call(
        functools.partial(smooth_kernel, nx, ny, nv),
        out_shape=(
            jax.ShapeDtypeStruct((nv, size_x + 2, size_y + 2, vecs, depth), F32),
            jax.ShapeDtypeStruct((size_x + 2, size_y + 2, 1, depth), F32),
            jax.ShapeDtypeStruct((size_x + 2, size_y + 2, 1, slots), jnp.int32),
        ),
        in_specs=[vmem] * 3,
        out_specs=(vmem,) * 3,
        scratch_shapes=[
            pltpu.VMEM((wide_x, wide_y, vecs, depth), F32),
            pltpu.VMEM((wide_x, wide_y, vecs, depth), F32),
            pltpu.VMEM((wide_x, wide_y, vecs, depth), F32),
            pltpu.VMEM((wide_x, wide_y, 1, depth), F32),
            pltpu.VMEM((wide_x, wide_y, 1, slots), jnp.int32),
            dma((8,)), dma((8,)), dma((8,)), dma((8,)), dma((8,)), dma((8,)),
            dma((nv, size_x + 2)), dma((nv, size_x + 2)),
        ],
        compiler_params=pltpu.CompilerParams(collective_id=0, has_side_effects=True),
        name="smooth",
    )(turned, conductivity[:, :, None, :], c_points[:, :, None, :])
    count = -(-cols // GROUP)
    rows = GROUP * slots
    more = cols + 2 * GROUP
    interp, coarse = pl.pallas_call(
        functools.partial(coarse_kernel, size_x, size_y, slots),
        out_shape=(
            jax.ShapeDtypeStruct((size_x, size_y, slots, depth), F32),
            jax.ShapeDtypeStruct((size_x, 9, size_y, slots * slots), F32),
        ),
        in_specs=[vmem] * 3,
        out_specs=(vmem, vmem),
        scratch_shapes=[
            pltpu.VMEM((count, rows, depth), F32),
            pltpu.VMEM((count, rows, depth), F32),
            pltpu.VMEM((count, slots, rows), F32),
            pltpu.VMEM((more, slots, depth), BF16),
            pltpu.VMEM((more, slots, depth), BF16),
            pltpu.VMEM((more, slots, depth), BF16),
            pltpu.VMEM((more, slots, depth), BF16),
            pltpu.VMEM((more, slots, depth), F32),
        ],
        name="coarse",
    )(
        field.reshape(nv, cols, vecs, depth),
        knots.reshape(cols, 1, depth),
        spots.reshape(cols, 1, slots),
    )
    return interp, jnp.transpose(coarse, (0, 2, 1, 3))


def solution(mesh):
    placed = (P("vert", "gx", "gy", None), P("gx", "gy", None), P("gx", "gy", None))
    return jax.shard_map(
        functools.partial(body, mesh.shape["gx"], mesh.shape["gy"], mesh.shape["vert"]),
        mesh=mesh,
        in_specs=placed,
        out_specs=(P("gx", "gy", None, None), P("gx", "gy", None, None)),
        check_vma=False,
    )
```

```python
import functools

import jax
import jax.numpy as jnp
from jax import lax
from jax.experimental import pallas as pl
from jax.experimental.pallas import tpu as pltpu
from jax.sharding import PartitionSpec as P

SWEEPS = 3
ANISOTROPY = (1.0, 0.6, 0.15)
OMEGA = 0.6
SHIFT = 0.5
RIDGE = 0.1
HALO = SWEEPS
GROUP = 8
UNROLL = True
MESH = pl.DeviceIdType.MESH
F32 = jnp.float32
BF16 = jnp.bfloat16


def smear_z(x):
    axis = x.ndim - 1
    depth = x.shape[axis]
    lane = lax.broadcasted_iota(jnp.int32, x.shape, axis)
    below = jnp.where(lane == 0, 0.0, pltpu.roll(x, 1, axis))
    above = jnp.where(lane == depth - 1, 0.0, pltpu.roll(x, depth - 1, axis))
    return x + ANISOTROPY[2] * (below + above)


def smear_xy(ref, row, col, pick):
    return pick(ref, row, col) + ANISOTROPY[0] * (pick(ref, row - 1, col) + pick(ref, row + 1, col))


def smear_row(ref, row, first, last, pick):
    across = {col: smear_xy(ref, row, col, pick) for col in range(first - 1, last + 1)}
    return [
        smear_z(across[col] + ANISOTROPY[1] * (across[col - 1] + across[col + 1]))
        for col in range(first, last)
    ]


def span(move, size):
    if move == 0:
        return pl.ds(0, size), pl.ds(HALO, size)
    if move > 0:
        return pl.ds(size - HALO, HALO), pl.ds(0, HALO)
    return pl.ds(0, HALO), pl.ds(size + HALO, HALO)


def hole(move, size):
    if move == 0:
        return pl.ds(HALO, size)
    return pl.ds(size + HALO, HALO) if move > 0 else pl.ds(0, HALO)


def rim(move, size):
    if move == 0:
        return pl.ds(1, size)
    return pl.ds(size + 1, 1) if move > 0 else pl.ds(0, 1)


def smooth_kernel(
    nx, ny, nv, v_ref, k_ref, c_ref, out_ref, knots_ref, spots_ref,
    one, two, gain, wide_k, wide_c, ksend, krecv, csend, crecv, vsend, vrecv,
    fsend, frecv, hsend, hrecv,
):
    size_x, size_y, vecs, depth = v_ref.shape
    wide_x, wide_y = size_x + 2 * HALO, size_y + 2 * HALO
    gx, gy, gv = lax.axis_index("gx"), lax.axis_index("gy"), lax.axis_index("vert")
    moves = [(mx, my) for mx in (-1, 0, 1) for my in (-1, 0, 1) if (mx, my) != (0, 0)]

    def inside(mx, my):
        ok_x = jnp.logical_and(gx + mx >= 0, gx + mx < nx)
        ok_y = jnp.logical_and(gy + my >= 0, gy + my < ny)
        return jnp.logical_and(ok_x, ok_y)

    barrier = pltpu.get_barrier_semaphore()
    total = jnp.int32(nv - 1)
    for mx, my in moves:
        here = inside(mx, my)

        @pl.when(here)
        def _():
            pl.semaphore_signal(
                barrier, inc=1, device_id=(gx + mx, gy + my, gv), device_id_type=MESH
            )

        total = total + here.astype(jnp.int32)
    for step in range(1, nv):
        pl.semaphore_signal(
            barrier, inc=1, device_id=(gx, gy, lax.rem(gv + step, nv)), device_id_type=MESH
        )
    pl.semaphore_wait(barrier, total)

    kinds = (
        (k_ref, wide_k, ksend, krecv), (v_ref, one, vsend, vrecv), (c_ref, wide_c, csend, crecv),
    )

    def departure(kind, no):
        mx, my = moves[no]
        source, target, send, recv = kinds[kind]
        from_x, to_x = span(mx, size_x)
        from_y, to_y = span(my, size_y)
        return pltpu.make_async_remote_copy(
            src_ref=source.at[from_x, from_y], dst_ref=target.at[to_x, to_y],
            send_sem=send.at[no], recv_sem=recv.at[no],
            device_id=(gx + mx, gy + my, gv), device_id_type=MESH,
        )

    def arrival(kind, no):
        mx, my = moves[no]
        other = moves.index((-mx, -my))
        _, target, send, recv = kinds[kind]
        place = target.at[hole(mx, size_x), hole(my, size_y)]
        return pltpu.make_async_remote_copy(
            src_ref=place, dst_ref=place, send_sem=send.at[other], recv_sem=recv.at[other],
            device_id=(gx + mx, gy + my, gv), device_id_type=MESH,
        )

    for no, (mx, my) in enumerate(moves):

        @pl.when(inside(mx, my))
        def _():
            for kind in range(3):
                departure(kind, no).start()

        @pl.when(jnp.logical_not(inside(mx, my)))
        def _():
            at_x, at_y = hole(mx, size_x), hole(my, size_y)
            for source, target, _, _ in kinds:
                target[at_x, at_y] = jnp.zeros(
                    (at_x.size, at_y.size) + source.shape[2:], source.dtype
                )
            rim_x, rim_y = rim(mx, size_x), rim(my, size_y)
            out_ref[:, rim_x, rim_y] = jnp.zeros((nv, rim_x.size, rim_y.size, vecs, depth), F32)

    for source, target, _, _ in kinds:
        target[pl.ds(HALO, size_x), pl.ds(HALO, size_y)] = source[...]

    for no, (mx, my) in enumerate(moves):

        @pl.when(inside(mx, my))
        def _():
            arrival(0, no).wait_recv()

    def pick_k(ref, row, col):
        return ref[row, col, 0:1, :]

    def pick_u(ref, row, col):
        return ref[row, col]

    def gains(row, carry):
        around = smear_row(wide_k, row, 1, wide_y - 1, pick_k)
        for col in range(1, wide_y - 1):
            mid = pick_k(wide_k, row, col)
            below = around[col - 1] - (1.0 - SHIFT) * mid
            alive = mid > 0.0
            value = jnp.where(alive, OMEGA * mid / jnp.where(alive, below, 1.0), 0.0)
            gain[row, col] = jnp.broadcast_to(value, (vecs, depth))
        return carry

    lax.fori_loop(1, wide_x - 1, gains, 0)

    for no, (mx, my) in enumerate(moves):

        @pl.when(inside(mx, my))
        def _():
            arrival(1, no).wait_recv()
            arrival(2, no).wait_recv()

    def scale(row, carry):
        for col in range(wide_y):
            one[row, col] = one[row, col] * jnp.broadcast_to(pick_k(wide_k, row, col), (vecs, depth))
        return carry

    lax.fori_loop(0, wide_x, scale, 0)

    def relaxed(ref, row, first, last):
        around = smear_row(ref, row, first, last, pick_u)
        result = []
        for col in range(first, last):
            factor = gain[row, col]
            result.append((1.0 - OMEGA - factor) * ref[row, col] + factor * around[col - first])
        return result

    source, target = one, two
    for sweep in range(1, SWEEPS):

        def step(row, carry, source=source, target=target, sweep=sweep):
            for no, value in enumerate(relaxed(source, row, sweep, wide_y - sweep)):
                target[row, sweep + no] = value
            return carry

        lax.fori_loop(sweep, wide_x - sweep, step, 0)
        source, target = target, source

    def last_sweep(row, carry):
        for no, value in enumerate(relaxed(source, row, SWEEPS, wide_y - SWEEPS)):
            out_ref[gv, row - SWEEPS + 1, no + 1] = value
        return carry

    lax.fori_loop(SWEEPS, wide_x - SWEEPS, last_sweep, 0)

    pieces = (
        (pl.ds(1, 1), pl.ds(1, size_y)),
        (pl.ds(size_x, 1), pl.ds(1, size_y)),
        (pl.ds(2, size_x - 2), pl.ds(1, 1)),
        (pl.ds(2, size_x - 2), pl.ds(size_y, 1)),
        (pl.ds(2, size_x - 2), pl.ds(2, size_y - 2)),
    )

    def piece_copy(no, step, half):
        place = out_ref.at[(half,) + pieces[no]]
        return pltpu.make_async_remote_copy(
            src_ref=place, dst_ref=place,
            send_sem=fsend.at[step - 1, no], recv_sem=frecv.at[step - 1, no],
            device_id=(gx, gy, lax.rem(gv + step, nv)), device_id_type=MESH,
        )

    def edge(move, size):
        if move == 0:
            return pl.ds(1, size), pl.ds(1, size)
        if move > 0:
            return pl.ds(size, 1), pl.ds(0, 1)
        return pl.ds(1, 1), pl.ds(size + 1, 1)

    def rim_departure(step, half, no):
        mx, my = moves[no]
        from_x, to_x = edge(mx, size_x)
        from_y, to_y = edge(my, size_y)
        return pltpu.make_async_remote_copy(
            src_ref=out_ref.at[half, from_x, from_y], dst_ref=out_ref.at[half, to_x, to_y],
            send_sem=hsend.at[step, no], recv_sem=hrecv.at[step, no],
            device_id=(gx + mx, gy + my, gv), device_id_type=MESH,
        )

    def rim_arrival(step, half, no):
        mx, my = moves[no]
        other = moves.index((-mx, -my))
        place = out_ref.at[half, edge(-mx, size_x)[1], edge(-my, size_y)[1]]
        return pltpu.make_async_remote_copy(
            src_ref=place, dst_ref=place,
            send_sem=hsend.at[step, other], recv_sem=hrecv.at[step, other],
            device_id=(gx + mx, gy + my, gv), device_id_type=MESH,
        )

    for no in range(len(pieces)):
        for step in range(1, nv):
            piece_copy(no, step, gv).start()
    for step in range(nv):
        half = lax.rem(gv - step + nv, nv)
        if step > 0:
            for no in range(len(pieces) - 1):
                piece_copy(no, step, half).wait_recv()
        for no, (mx, my) in enumerate(moves):

            @pl.when(inside(mx, my))
            def _():
                rim_departure(step, half, no).start()

    rim_x, rim_y = pl.ds(HALO - 1, size_x + 2), pl.ds(HALO - 1, size_y + 2)
    knots_ref[...] = wide_k[rim_x, rim_y]
    spots_ref[...] = wide_c[rim_x, rim_y]

    for step in range(1, nv):
        piece_copy(len(pieces) - 1, step, lax.rem(gv - step + nv, nv)).wait_recv()
        for no in range(len(pieces)):
            piece_copy(no, step, gv).wait_send()
    for no, (mx, my) in enumerate(moves):

        @pl.when(inside(mx, my))
        def _():
            for kind in range(3):
                departure(kind, no).wait_send()
            for step in range(nv):
                half = lax.rem(gv - step + nv, nv)
                rim_arrival(step, half, no).wait_recv()
                rim_departure(step, half, no).wait_send()


def split(x):
    high = x.astype(BF16)
    return high, (x - high.astype(F32)).astype(BF16)


NT = (((1,), (1,)), ((), ()))
NN = (((1,), (0,)), ((), ()))


def dot(a, b, dims):
    return lax.dot_general(a, b, dims, preferred_element_type=F32)


def dot3(a, b, dims):
    return dot(a[0], b[0], dims) + dot(a[0], b[1], dims) + dot(a[1], b[0], dims)


def coarse_kernel(
    size_x, size_y, slots, f_ref, k_ref, c_ref, interp_ref, coarse_ref,
    hot, right_s, gram_s, lh, ll, rh, rl, ch,
):
    nv, cols, vecs, depth = f_ref.shape
    wide_y = size_y + 2
    rows = GROUP * slots
    members = GROUP * nv * vecs
    count = gram_s.shape[0]
    padded = -(-wide_y // GROUP) * GROUP
    band = size_y * slots

    def lanes(shape):
        return lax.broadcasted_iota(jnp.int32, shape, len(shape) - 1)

    def subs(shape):
        return lax.broadcasted_iota(jnp.int32, shape, len(shape) - 2)

    same = subs((rows, members)) // slots == lanes((rows, members)) // (nv * vecs)
    same_slots = subs((rows, rows)) // slots == lanes((rows, rows)) // slots
    own_lane = subs((rows, slots)) % slots == lanes((rows, slots))
    ones = jnp.ones((slots, depth), BF16)

    def start_of(no):
        return jnp.minimum(no * GROUP, cols - GROUP)

    def gather(no, carry):
        start = start_of(no)
        knots = k_ref[pl.ds(start, GROUP)]
        alive = knots > 0.0
        inverse = jnp.where(alive, 1.0 / jnp.where(alive, knots, 1.0), 0.0)
        field = jnp.concatenate(
            [f_ref[half, pl.ds(start, GROUP)] * inverse for half in range(nv)], axis=1
        ).reshape(members, depth)
        spots = jnp.broadcast_to(
            c_ref[pl.ds(start, GROUP)].astype(F32), (GROUP, slots, slots)
        ).reshape(rows, slots)
        spread = dot(jnp.where(own_lane, spots, 0.0).astype(BF16), ones, NN)
        onehot = jnp.where(spread == lanes((rows, depth)).astype(F32), 1.0, 0.0)
        hot[no] = onehot
        fh, fl = split(field)
        picked = onehot.astype(BF16)
        cvals = jnp.where(same, dot(picked, fh, NT) + dot(picked, fl, NT), 0.0)
        pair = split(cvals)
        right_s[no] = dot3(pair, (fh, fl), NN)
        gram = dot3(pair, pair, NT)
        gram_s[no] = jnp.sum(gram.reshape(GROUP, slots, rows), axis=0)
        return carry

    lax.fori_loop(0, count, gather, 0, unroll=UNROLL)

    shape = (count, slots, rows)
    lane = lanes(shape) % slots
    sub = subs(shape)
    system = gram_s[...]
    diagonal = jnp.sum(jnp.where(lane == sub, system, 0.0), axis=1)
    block = jnp.where(same_slots, 1.0, 0.0).astype(BF16)
    first = diagonal.astype(BF16)
    rest = diagonal - first.astype(F32)
    second = rest.astype(BF16)
    third = (rest - second.astype(F32)).astype(BF16)
    trace = dot(first, block, NN) + dot(second, block, NN) + dot(third, block, NN)
    ridge = RIDGE * trace / slots + 1e-06
    system = system + jnp.where(lane == sub, ridge[:, None, :], 0.0)
    flat = (count * slots, rows)
    base = lanes(flat) // slots * slots
    for pivot in range(slots):
        column = jnp.take_along_axis(
            system.reshape(flat), base + pivot, axis=1, mode="promise_in_bounds"
        ).reshape(shape)
        line = system[:, pivot : pivot + 1, :]
        here = lane[:, 0:1, :] == pivot
        line = jnp.where(here, 1.0, line) / column[:, pivot : pivot + 1, :]
        system = jnp.where(
            sub == pivot, line, jnp.where(lane == pivot, 0.0, system) - column * line
        )
    gram_s[...] = system

    def weigh(no, carry):
        start = start_of(no)
        inverse = jnp.where(
            same_slots,
            jnp.broadcast_to(gram_s[no][None], (GROUP, slots, rows)).reshape(rows, rows),
            0.0,
        )
        weights = dot3(split(inverse), split(right_s[no]), NN).reshape(GROUP, slots, depth)
        onehot = hot[no].reshape(GROUP, slots, depth)
        crow = jnp.sum(onehot, axis=1, keepdims=True)
        value = weights * (1.0 - crow) + onehot
        hot_cols = pl.ds(start, GROUP)
        ch[hot_cols] = value
        left = value * k_ref[hot_cols]
        high, low = split(left.reshape(rows, depth))
        lh[hot_cols] = high.reshape(GROUP, slots, depth)
        ll[hot_cols] = low.reshape(GROUP, slots, depth)
        high, low = split(smear_z(left.reshape(rows, depth)))
        rh[hot_cols] = high.reshape(GROUP, slots, depth)
        rl[hot_cols] = low.reshape(GROUP, slots, depth)
        return carry

    lax.fori_loop(0, count, weigh, 0, unroll=UNROLL)

    half = GROUP * slots
    groups = slots * slots // half
    tall = (GROUP, half)
    pick_row = lanes(tall) // slots
    out_row = subs(tall)

    def merge(tiles):
        hop = GROUP // 2
        while hop >= 1:
            up = out_row // hop % 2 == 1
            straight = up == (pick_row // hop % 2 == 1)
            merged = []
            for no in range(hop):
                one, two = tiles[no], tiles[no + hop]
                same_place = jnp.where(up, two, one)
                moved = jnp.where(up, one, two)
                down = pltpu.roll(moved, hop, 0)
                if 2 * hop != GROUP:
                    down = jnp.where(up, down, pltpu.roll(moved, GROUP - hop, 0))
                merged.append(jnp.where(straight, same_place, down))
            tiles = merged
            hop //= 2
        return tiles[0]

    block_lane = lanes((slots, half)) % slots

    def galerkin(row, carry):
        at = (row + 1) * wide_y
        mine = pl.ds(at + 1, size_y)
        own = ch[mine]
        interp_ref[row] = own
        across = k_ref[pl.ds(at, wide_y)] + ANISOTROPY[0] * (
            k_ref[pl.ds(at - wide_y, wide_y)] + k_ref[pl.ds(at + wide_y, wide_y)]
        )
        along = across[1 : size_y + 1] + ANISOTROPY[1] * (across[0:size_y] + across[2:])
        whole = smear_z(along.reshape(size_y, depth)).reshape(size_y, 1, depth)
        left = (lh[mine].reshape(band, depth), ll[mine].reshape(band, depth))
        right = rh[mine].astype(F32) + rl[mine].astype(F32)
        centre = right - own * (whole + SHIFT * k_ref[mine])
        middle = dot3(left, split(centre.reshape(band, depth)), NT)
        for move_x in (-1, 0, 1):
            there = pl.ds(at + move_x * wide_y, padded)
            other = (
                rh[there].reshape(padded * slots, depth),
                rl[there].reshape(padded * slots, depth),
            )
            product = dot3(left, other, NT)
            for move_y in (-1, 0, 1):
                weight = 1.0
                if move_x != 0:
                    weight = weight * ANISOTROPY[0]
                if move_y != 0:
                    weight = weight * ANISOTROPY[1]
                order = 3 * (move_x + 1) + move_y + 1
                for chunk in range(0, size_y, GROUP):
                    spread = []
                    for col in range(chunk, chunk + GROUP):
                        central = move_x == 0 and move_y == 0
                        origin = middle if central else product
                        place = col if central else col + 1 + move_y
                        first_lane = place // GROUP * half
                        values = origin[
                            col * slots : (col + 1) * slots, first_lane : first_lane + half
                        ]
                        spread.append(
                            jnp.take_along_axis(
                                values, block_lane + place % GROUP * slots, axis=1,
                                mode="promise_in_bounds",
                            )
                        )
                    parts = [
                        merge([tile[g * GROUP : (g + 1) * GROUP] for tile in spread])
                        for g in range(groups)
                    ]
                    coarse_ref[row, order, chunk : chunk + GROUP, :] = -weight * jnp.concatenate(
                        parts, axis=1
                    )
        return carry

    lax.fori_loop(0, size_x, galerkin, 0)


def body(nx, ny, nv, vectors, conductivity, c_points):
    vecs, size_x, size_y, depth = vectors.shape
    slots = c_points.shape[-1]
    turned = jnp.transpose(vectors, (1, 2, 0, 3))
    wide_x, wide_y = size_x + 2 * HALO, size_y + 2 * HALO
    cols = (size_x + 2) * (size_y + 2)
    vmem = pl.BlockSpec(memory_space=pltpu.VMEM)
    dma = pltpu.SemaphoreType.DMA
    field, knots, spots = pl.pallas_call(
        functools.partial(smooth_kernel, nx, ny, nv),
        out_shape=(
            jax.ShapeDtypeStruct((nv, size_x + 2, size_y + 2, vecs, depth), F32),
            jax.ShapeDtypeStruct((size_x + 2, size_y + 2, 1, depth), F32),
            jax.ShapeDtypeStruct((size_x + 2, size_y + 2, 1, slots), jnp.int32),
        ),
        in_specs=[vmem] * 3,
        out_specs=(vmem,) * 3,
        scratch_shapes=[
            pltpu.VMEM((wide_x, wide_y, vecs, depth), F32),
            pltpu.VMEM((wide_x, wide_y, vecs, depth), F32),
            pltpu.VMEM((wide_x, wide_y, vecs, depth), F32),
            pltpu.VMEM((wide_x, wide_y, 1, depth), F32),
            pltpu.VMEM((wide_x, wide_y, 1, slots), jnp.int32),
            dma((8,)), dma((8,)), dma((8,)), dma((8,)), dma((8,)), dma((8,)),
            dma((nv, 5)), dma((nv, 5)), dma((nv, 8)), dma((nv, 8)),
        ],
        compiler_params=pltpu.CompilerParams(collective_id=0, has_side_effects=True),
        name="smooth",
    )(turned, conductivity[:, :, None, :], c_points[:, :, None, :])
    count = -(-cols // GROUP)
    rows = GROUP * slots
    more = cols + 2 * GROUP
    interp, coarse = pl.pallas_call(
        functools.partial(coarse_kernel, size_x, size_y, slots),
        out_shape=(
            jax.ShapeDtypeStruct((size_x, size_y, slots, depth), F32),
            jax.ShapeDtypeStruct((size_x, 9, size_y, slots * slots), F32),
        ),
        in_specs=[vmem] * 3,
        out_specs=(vmem, vmem),
        scratch_shapes=[
            pltpu.VMEM((count, rows, depth), F32),
            pltpu.VMEM((count, rows, depth), F32),
            pltpu.VMEM((count, slots, rows), F32),
            pltpu.VMEM((more, slots, depth), BF16),
            pltpu.VMEM((more, slots, depth), BF16),
            pltpu.VMEM((more, slots, depth), BF16),
            pltpu.VMEM((more, slots, depth), BF16),
            pltpu.VMEM((more, slots, depth), F32),
        ],
        name="coarse",
    )(
        field.reshape(nv, cols, vecs, depth),
        knots.reshape(cols, 1, depth),
        spots.reshape(cols, 1, slots),
    )
    return interp, jnp.transpose(coarse, (0, 2, 1, 3))


def solution(mesh):
    placed = (P("vert", "gx", "gy", None), P("gx", "gy", None), P("gx", "gy", None))
    return jax.shard_map(
        functools.partial(body, mesh.shape["gx"], mesh.shape["gy"], mesh.shape["vert"]),
        mesh=mesh,
        in_specs=placed,
        out_specs=(P("gx", "gy", None, None), P("gx", "gy", None, None)),
        check_vma=False,
    )
```

```python
import functools

import jax
import jax.numpy as jnp
from jax import lax
from jax.experimental import pallas as pl
from jax.experimental.pallas import tpu as pltpu
from jax.sharding import PartitionSpec as P

SWEEPS = 3
ANISOTROPY = (1.0, 0.6, 0.15)
OMEGA = 0.6
SHIFT = 0.5
RIDGE = 0.1
HALO = SWEEPS
GROUP = 8
BATCH = 7
BATCH_2 = 2
ROWS = True
MESH = pl.DeviceIdType.MESH
F32 = jnp.float32
BF16 = jnp.bfloat16


def smear_z(x):
    axis = x.ndim - 1
    depth = x.shape[axis]
    lane = lax.broadcasted_iota(jnp.int32, x.shape, axis)
    below = jnp.where(lane == 0, 0.0, pltpu.roll(x, 1, axis))
    above = jnp.where(lane == depth - 1, 0.0, pltpu.roll(x, depth - 1, axis))
    return x + ANISOTROPY[2] * (below + above)


def smear_xy(ref, row, col, pick):
    return pick(ref, row, col) + ANISOTROPY[0] * (pick(ref, row - 1, col) + pick(ref, row + 1, col))


def smear_row(ref, row, first, last, pick):
    across = {col: smear_xy(ref, row, col, pick) for col in range(first - 1, last + 1)}
    return [
        smear_z(across[col] + ANISOTROPY[1] * (across[col - 1] + across[col + 1]))
        for col in range(first, last)
    ]


def span(move, size):
    if move == 0:
        return pl.ds(0, size), pl.ds(HALO, size)
    if move > 0:
        return pl.ds(size - HALO, HALO), pl.ds(0, HALO)
    return pl.ds(0, HALO), pl.ds(size + HALO, HALO)


def hole(move, size):
    if move == 0:
        return pl.ds(HALO, size)
    return pl.ds(size + HALO, HALO) if move > 0 else pl.ds(0, HALO)


def rim(move, size):
    if move == 0:
        return pl.ds(1, size)
    return pl.ds(size + 1, 1) if move > 0 else pl.ds(0, 1)


def smooth_kernel(
    nx, ny, nv, raw_ref, k_ref, c_ref, out_ref, knots_ref, spots_ref,
    one, two, gain, wide_k, wide_c, ksend, krecv, csend, crecv, vsend, vrecv,
    fsend, frecv, hsend, hrecv, v_ref, turn,
):
    size_x, size_y, vecs, depth = v_ref.shape
    wide_x, wide_y = size_x + 2 * HALO, size_y + 2 * HALO
    gx, gy, gv = lax.axis_index("gx"), lax.axis_index("gy"), lax.axis_index("vert")
    moves = [(mx, my) for mx in (-1, 0, 1) for my in (-1, 0, 1) if (mx, my) != (0, 0)]

    def inside(mx, my):
        ok_x = jnp.logical_and(gx + mx >= 0, gx + mx < nx)
        ok_y = jnp.logical_and(gy + my >= 0, gy + my < ny)
        return jnp.logical_and(ok_x, ok_y)

    turns = [
        pltpu.make_async_copy(raw_ref.at[vec], v_ref.at[:, :, vec], turn.at[vec])
        for vec in range(vecs)
    ]
    for copy in turns:
        copy.start()

    barrier = pltpu.get_barrier_semaphore()
    total = jnp.int32(nv - 1)
    for mx, my in moves:
        here = inside(mx, my)

        @pl.when(here)
        def _():
            pl.semaphore_signal(
                barrier, inc=1, device_id=(gx + mx, gy + my, gv), device_id_type=MESH
            )

        total = total + here.astype(jnp.int32)
    for step in range(1, nv):
        pl.semaphore_signal(
            barrier, inc=1, device_id=(gx, gy, lax.rem(gv + step, nv)), device_id_type=MESH
        )
    pl.semaphore_wait(barrier, total)

    kinds = (
        (k_ref, wide_k, ksend, krecv), (v_ref, one, vsend, vrecv), (c_ref, wide_c, csend, crecv),
    )

    def departure(kind, no):
        mx, my = moves[no]
        source, target, send, recv = kinds[kind]
        from_x, to_x = span(mx, size_x)
        from_y, to_y = span(my, size_y)
        return pltpu.make_async_remote_copy(
            src_ref=source.at[from_x, from_y], dst_ref=target.at[to_x, to_y],
            send_sem=send.at[no], recv_sem=recv.at[no],
            device_id=(gx + mx, gy + my, gv), device_id_type=MESH,
        )

    def arrival(kind, no):
        mx, my = moves[no]
        other = moves.index((-mx, -my))
        _, target, send, recv = kinds[kind]
        place = target.at[hole(mx, size_x), hole(my, size_y)]
        return pltpu.make_async_remote_copy(
            src_ref=place, dst_ref=place, send_sem=send.at[other], recv_sem=recv.at[other],
            device_id=(gx + mx, gy + my, gv), device_id_type=MESH,
        )

    for no, (mx, my) in enumerate(moves):

        @pl.when(inside(mx, my))
        def _():
            departure(0, no).start()

        @pl.when(jnp.logical_not(inside(mx, my)))
        def _():
            at_x, at_y = hole(mx, size_x), hole(my, size_y)
            for source, target, _, _ in kinds:
                target[at_x, at_y] = jnp.zeros(
                    (at_x.size, at_y.size) + source.shape[2:], source.dtype
                )
            rim_x, rim_y = rim(mx, size_x), rim(my, size_y)
            out_ref[:, rim_x, rim_y] = jnp.zeros((nv, rim_x.size, rim_y.size, vecs, depth), F32)

    for copy in turns:
        copy.wait()
    for kind in (1, 2):
        for no, (mx, my) in enumerate(moves):

            @pl.when(inside(mx, my))
            def _():
                departure(kind, no).start()

    for source, target, _, _ in kinds:
        target[pl.ds(HALO, size_x), pl.ds(HALO, size_y)] = source[...]

    for no, (mx, my) in enumerate(moves):

        @pl.when(inside(mx, my))
        def _():
            arrival(0, no).wait_recv()

    def pick_k(ref, row, col):
        return ref[row, col, 0:1, :]

    def pick_u(ref, row, col):
        return ref[row, col]

    def gains(row, carry):
        around = smear_row(wide_k, row, 1, wide_y - 1, pick_k)
        for col in range(1, wide_y - 1):
            mid = pick_k(wide_k, row, col)
            below = around[col - 1] - (1.0 - SHIFT) * mid
            alive = mid > 0.0
            value = jnp.where(alive, OMEGA * mid / jnp.where(alive, below, 1.0), 0.0)
            gain[row, col] = jnp.broadcast_to(value, (vecs, depth))
        return carry

    lax.fori_loop(1, wide_x - 1, gains, 0)

    for no, (mx, my) in enumerate(moves):

        @pl.when(inside(mx, my))
        def _():
            arrival(1, no).wait_recv()
            arrival(2, no).wait_recv()

    def scale(row, carry):
        for col in range(wide_y):
            one[row, col] = one[row, col] * jnp.broadcast_to(pick_k(wide_k, row, col), (vecs, depth))
        return carry

    lax.fori_loop(0, wide_x, scale, 0)

    def relaxed(ref, row, first, last):
        around = smear_row(ref, row, first, last, pick_u)
        result = []
        for col in range(first, last):
            factor = gain[row, col]
            result.append((1.0 - OMEGA - factor) * ref[row, col] + factor * around[col - first])
        return result

    source, target = one, two
    for sweep in range(1, SWEEPS):

        def step(row, carry, source=source, target=target, sweep=sweep):
            for no, value in enumerate(relaxed(source, row, sweep, wide_y - sweep)):
                target[row, sweep + no] = value
            return carry

        lax.fori_loop(sweep, wide_x - sweep, step, 0)
        source, target = target, source

    def last_sweep(row, carry):
        for no, value in enumerate(relaxed(source, row, SWEEPS, wide_y - SWEEPS)):
            out_ref[gv, row - SWEEPS + 1, no + 1] = value
        return carry

    lax.fori_loop(SWEEPS, wide_x - SWEEPS, last_sweep, 0)

    pieces = (
        (pl.ds(1, 1), pl.ds(1, size_y)),
        (pl.ds(size_x, 1), pl.ds(1, size_y)),
        (pl.ds(2, size_x - 2), pl.ds(1, 1)),
        (pl.ds(2, size_x - 2), pl.ds(size_y, 1)),
        (pl.ds(2, size_x - 2), pl.ds(2, size_y - 2)),
    )

    def piece_copy(no, step, half):
        place = out_ref.at[(half,) + pieces[no]]
        return pltpu.make_async_remote_copy(
            src_ref=place, dst_ref=place,
            send_sem=fsend.at[step - 1, no], recv_sem=frecv.at[step - 1, no],
            device_id=(gx, gy, lax.rem(gv + step, nv)), device_id_type=MESH,
        )

    def edge(move, size):
        if move == 0:
            return pl.ds(1, size), pl.ds(1, size)
        if move > 0:
            return pl.ds(size, 1), pl.ds(0, 1)
        return pl.ds(1, 1), pl.ds(size + 1, 1)

    def rim_departure(step, half, no):
        mx, my = moves[no]
        from_x, to_x = edge(mx, size_x)
        from_y, to_y = edge(my, size_y)
        return pltpu.make_async_remote_copy(
            src_ref=out_ref.at[half, from_x, from_y], dst_ref=out_ref.at[half, to_x, to_y],
            send_sem=hsend.at[step, no], recv_sem=hrecv.at[step, no],
            device_id=(gx + mx, gy + my, gv), device_id_type=MESH,
        )

    def rim_arrival(step, half, no):
        mx, my = moves[no]
        other = moves.index((-mx, -my))
        place = out_ref.at[half, edge(-mx, size_x)[1], edge(-my, size_y)[1]]
        return pltpu.make_async_remote_copy(
            src_ref=place, dst_ref=place,
            send_sem=hsend.at[step, other], recv_sem=hrecv.at[step, other],
            device_id=(gx + mx, gy + my, gv), device_id_type=MESH,
        )

    for no in range(len(pieces)):
        for step in range(1, nv):
            piece_copy(no, step, gv).start()
    for step in range(nv):
        half = lax.rem(gv - step + nv, nv)
        if step > 0:
            for no in range(len(pieces) - 1):
                piece_copy(no, step, half).wait_recv()
        for no, (mx, my) in enumerate(moves):

            @pl.when(inside(mx, my))
            def _():
                rim_departure(step, half, no).start()

    rim_x, rim_y = pl.ds(HALO - 1, size_x + 2), pl.ds(HALO - 1, size_y + 2)
    knots_ref[...] = wide_k[rim_x, rim_y]
    spots_ref[...] = wide_c[rim_x, rim_y]

    for step in range(1, nv):
        piece_copy(len(pieces) - 1, step, lax.rem(gv - step + nv, nv)).wait_recv()
        for no in range(len(pieces)):
            piece_copy(no, step, gv).wait_send()
    for no, (mx, my) in enumerate(moves):

        @pl.when(inside(mx, my))
        def _():
            for kind in range(3):
                departure(kind, no).wait_send()
            for step in range(nv):
                half = lax.rem(gv - step + nv, nv)
                rim_arrival(step, half, no).wait_recv()
                rim_departure(step, half, no).wait_send()


def split(x):
    high = x.astype(BF16)
    return high, (x - high.astype(F32)).astype(BF16)


NT = (((1,), (1,)), ((), ()))
NN = (((1,), (0,)), ((), ()))


def dot(a, b, dims):
    return lax.dot_general(a, b, dims, preferred_element_type=F32)


def dot3(a, b, dims):
    return dot(a[0], b[0], dims) + dot(a[0], b[1], dims) + dot(a[1], b[0], dims)


def coarse_kernel(
    size_x, size_y, slots, f_ref, k_ref, c_ref, interp_ref, coarse_ref,
    hot, right_h, right_l, gram_s, lh, ll, rh, rl, ch,
):
    nv, cols, vecs, depth = f_ref.shape
    wide_y = size_y + 2
    rows = GROUP * slots
    members = GROUP * nv * vecs
    count = gram_s.shape[0]
    padded = -(-wide_y // GROUP) * GROUP
    band = size_y * slots

    def lanes(shape):
        return lax.broadcasted_iota(jnp.int32, shape, len(shape) - 1)

    def subs(shape):
        return lax.broadcasted_iota(jnp.int32, shape, len(shape) - 2)

    same = subs((rows, members)) // slots == lanes((rows, members)) // (nv * vecs)
    same_slots = subs((rows, rows)) // slots == lanes((rows, rows)) // slots
    own_lane = subs((rows, slots)) % slots == lanes((rows, slots))
    ones = jnp.ones((slots, depth), BF16)

    def start_of(no):
        return jnp.minimum(no * GROUP, cols - GROUP)

    def gather(batch):
        fields, spreads = [], []
        for no in batch:
            start = min(no * GROUP, cols - GROUP)
            knots = k_ref[pl.ds(start, GROUP)]
            alive = knots > 0.0
            inverse = jnp.where(alive, 1.0 / jnp.where(alive, knots, 1.0), 0.0)
            field = jnp.concatenate(
                [f_ref[half, pl.ds(start, GROUP)] * inverse for half in range(nv)], axis=1
            ).reshape(members, depth)
            fields.append(split(field))
            spots = jnp.broadcast_to(
                c_ref[pl.ds(start, GROUP)].astype(F32), (GROUP, slots, slots)
            ).reshape(rows, slots)
            spreads.append(dot(jnp.where(own_lane, spots, 0.0).astype(BF16), ones, NN))
        pairs = []
        for no, spread, (high, low) in zip(batch, spreads, fields):
            onehot = jnp.where(spread == lanes((rows, depth)).astype(F32), 1.0, 0.0).astype(BF16)
            hot[no] = onehot
            pairs.append(dot(onehot, high, NT) + dot(onehot, low, NT))
        pairs = [split(jnp.where(same, cvals, 0.0)) for cvals in pairs]
        grams = [dot3(pair, pair, NT) for pair in pairs]
        rights = [dot3(pair, field, NN) for pair, field in zip(pairs, fields)]
        for no, gram, right in zip(batch, grams, rights):
            gram_s[no] = jnp.sum(gram.reshape(GROUP, slots, rows), axis=0)
            high, low = split(right)
            right_h[no] = high
            right_l[no] = low

    for first in range(0, count, BATCH):
        gather(range(first, min(first + BATCH, count)))

    shape = (count, slots, rows)
    lane = lanes(shape) % slots
    sub = subs(shape)
    system = gram_s[...]
    diagonal = jnp.sum(jnp.where(lane == sub, system, 0.0), axis=1)
    block = jnp.where(same_slots, 1.0, 0.0).astype(BF16)
    first = diagonal.astype(BF16)
    rest = diagonal - first.astype(F32)
    second = rest.astype(BF16)
    third = (rest - second.astype(F32)).astype(BF16)
    trace = dot(first, block, NN) + dot(second, block, NN) + dot(third, block, NN)
    ridge = RIDGE * trace / slots + 1e-06
    system = system + jnp.where(lane == sub, ridge[:, None, :], 0.0)
    flat = (count * slots, rows)
    base = lanes(flat) // slots * slots
    for pivot in range(slots):
        column = jnp.take_along_axis(
            system.reshape(flat), base + pivot, axis=1, mode="promise_in_bounds"
        ).reshape(shape)
        line = system[:, pivot : pivot + 1, :]
        here = lane[:, 0:1, :] == pivot
        line = jnp.where(here, 1.0, line) / column[:, pivot : pivot + 1, :]
        system = jnp.where(
            sub == pivot, line, jnp.where(lane == pivot, 0.0, system) - column * line
        )
    gram_s[...] = system

    def weigh(batch):
        inverses = [
            split(
                jnp.where(
                    same_slots,
                    jnp.broadcast_to(gram_s[no][None], (GROUP, slots, rows)).reshape(rows, rows),
                    0.0,
                )
            )
            for no in batch
        ]
        solved = [
            dot3(inverse, (right_h[no], right_l[no]), NN) for no, inverse in zip(batch, inverses)
        ]
        for no, weights in zip(batch, solved):
            here = pl.ds(min(no * GROUP, cols - GROUP), GROUP)
            onehot = hot[no].astype(F32).reshape(GROUP, slots, depth)
            crow = jnp.sum(onehot, axis=1, keepdims=True)
            value = weights.reshape(GROUP, slots, depth) * (1.0 - crow) + onehot
            ch[here] = value
            left = value * k_ref[here]
            high, low = split(left)
            lh[here] = high
            ll[here] = low
            high, low = split(smear_z(left.reshape(rows, depth)))
            rh[here] = high.reshape(GROUP, slots, depth)
            rl[here] = low.reshape(GROUP, slots, depth)

    for first in range(0, count, BATCH_2):
        weigh(range(first, min(first + BATCH_2, count)))

    half = GROUP * slots
    groups = slots * slots // half
    tall = (GROUP, half)
    pick_row = lanes(tall) // slots
    out_row = subs(tall)

    def merge(tiles):
        hop = GROUP // 2
        while hop >= 1:
            up = out_row // hop % 2 == 1
            straight = up == (pick_row // hop % 2 == 1)
            merged = []
            for no in range(hop):
                one, two = tiles[no], tiles[no + hop]
                same_place = jnp.where(up, two, one)
                moved = jnp.where(up, one, two)
                down = pltpu.roll(moved, hop, 0)
                if 2 * hop != GROUP:
                    down = jnp.where(up, down, pltpu.roll(moved, GROUP - hop, 0))
                merged.append(jnp.where(straight, same_place, down))
            tiles = merged
            hop //= 2
        return tiles[0]

    block_lane = lanes((slots, half)) % slots

    def galerkin(row, carry):
        at = (row + 1) * wide_y
        mine = pl.ds(at + 1, size_y)
        own = ch[mine]
        interp_ref[row] = own
        across = k_ref[pl.ds(at, wide_y)] + ANISOTROPY[0] * (
            k_ref[pl.ds(at - wide_y, wide_y)] + k_ref[pl.ds(at + wide_y, wide_y)]
        )
        along = across[1 : size_y + 1] + ANISOTROPY[1] * (across[0:size_y] + across[2:])
        whole = smear_z(along.reshape(size_y, depth)).reshape(size_y, 1, depth)
        left = (lh[mine].reshape(band, depth), ll[mine].reshape(band, depth))
        right = rh[mine].astype(F32) + rl[mine].astype(F32)
        centre = right - own * (whole + SHIFT * k_ref[mine])
        middle = dot3(left, split(centre.reshape(band, depth)), NT)
        for move_x in (-1, 0, 1):
            there = pl.ds(at + move_x * wide_y, padded)
            other = (
                rh[there].reshape(padded * slots, depth),
                rl[there].reshape(padded * slots, depth),
            )
            product = dot3(left, other, NT)
            for move_y in (-1, 0, 1):
                weight = 1.0
                if move_x != 0:
                    weight = weight * ANISOTROPY[0]
                if move_y != 0:
                    weight = weight * ANISOTROPY[1]
                order = 3 * (move_x + 1) + move_y + 1
                for chunk in range(0, size_y, GROUP):
                    spread = []
                    for col in range(chunk, chunk + GROUP):
                        central = move_x == 0 and move_y == 0
                        origin = middle if central else product
                        place = col if central else col + 1 + move_y
                        first_lane = place // GROUP * half
                        values = origin[
                            col * slots : (col + 1) * slots, first_lane : first_lane + half
                        ]
                        spread.append(
                            jnp.take_along_axis(
                                values, block_lane + place % GROUP * slots, axis=1,
                                mode="promise_in_bounds",
                            )
                        )
                    parts = [
                        merge([tile[g * GROUP : (g + 1) * GROUP] for tile in spread])
                        for g in range(groups)
                    ]
                    coarse_ref[row, order, chunk : chunk + GROUP, :] = -weight * jnp.concatenate(
                        parts, axis=1
                    )
        return carry

    lax.fori_loop(0, size_x, galerkin, 0, unroll=ROWS)


def body(nx, ny, nv, vectors, conductivity, c_points):
    vecs, size_x, size_y, depth = vectors.shape
    slots = c_points.shape[-1]
    wide_x, wide_y = size_x + 2 * HALO, size_y + 2 * HALO
    cols = (size_x + 2) * (size_y + 2)
    vmem = pl.BlockSpec(memory_space=pltpu.VMEM)
    dma = pltpu.SemaphoreType.DMA
    field, knots, spots = pl.pallas_call(
        functools.partial(smooth_kernel, nx, ny, nv),
        out_shape=(
            jax.ShapeDtypeStruct((nv, size_x + 2, size_y + 2, vecs, depth), F32),
            jax.ShapeDtypeStruct((size_x + 2, size_y + 2, 1, depth), F32),
            jax.ShapeDtypeStruct((size_x + 2, size_y + 2, 1, slots), jnp.int32),
        ),
        in_specs=[pl.BlockSpec(memory_space=pl.ANY), vmem, vmem],
        out_specs=(vmem,) * 3,
        scratch_shapes=[
            pltpu.VMEM((wide_x, wide_y, vecs, depth), F32),
            pltpu.VMEM((wide_x, wide_y, vecs, depth), F32),
            pltpu.VMEM((wide_x, wide_y, vecs, depth), F32),
            pltpu.VMEM((wide_x, wide_y, 1, depth), F32),
            pltpu.VMEM((wide_x, wide_y, 1, slots), jnp.int32),
            dma((8,)), dma((8,)), dma((8,)), dma((8,)), dma((8,)), dma((8,)),
            dma((nv, 5)), dma((nv, 5)), dma((nv, 8)), dma((nv, 8)),
            pltpu.VMEM((size_x, size_y, vecs, depth), F32), dma((vecs,)),
        ],
        compiler_params=pltpu.CompilerParams(collective_id=0, has_side_effects=True),
        name="smooth",
    )(vectors, conductivity[:, :, None, :], c_points[:, :, None, :])
    count = -(-cols // GROUP)
    rows = GROUP * slots
    more = cols + 2 * GROUP
    interp, coarse = pl.pallas_call(
        functools.partial(coarse_kernel, size_x, size_y, slots),
        out_shape=(
            jax.ShapeDtypeStruct((size_x, size_y, slots, depth), F32),
            jax.ShapeDtypeStruct((size_x, 9, size_y, slots * slots), F32),
        ),
        in_specs=[vmem] * 3,
        out_specs=(vmem, vmem),
        scratch_shapes=[
            pltpu.VMEM((count, rows, depth), BF16),
            pltpu.VMEM((count, rows, depth), BF16),
            pltpu.VMEM((count, rows, depth), BF16),
            pltpu.VMEM((count, slots, rows), F32),
            pltpu.VMEM((more, slots, depth), BF16),
            pltpu.VMEM((more, slots, depth), BF16),
            pltpu.VMEM((more, slots, depth), BF16),
            pltpu.VMEM((more, slots, depth), BF16),
            pltpu.VMEM((more, slots, depth), F32),
        ],
        name="coarse",
    )(
        field.reshape(nv, cols, vecs, depth),
        knots.reshape(cols, 1, depth),
        spots.reshape(cols, 1, slots),
    )
    return interp, jnp.transpose(coarse, (0, 2, 1, 3))


def solution(mesh):
    placed = (P("vert", "gx", "gy", None), P("gx", "gy", None), P("gx", "gy", None))
    return jax.shard_map(
        functools.partial(body, mesh.shape["gx"], mesh.shape["gy"], mesh.shape["vert"]),
        mesh=mesh,
        in_specs=placed,
        out_specs=(P("gx", "gy", None, None), P("gx", "gy", None, None)),
        check_vma=False,
    )
```

```python
import functools

import jax
import jax.numpy as jnp
from jax import lax
from jax.experimental import pallas as pl
from jax.experimental.pallas import tpu as pltpu
from jax.sharding import PartitionSpec as P

SWEEPS = 3
ANISOTROPY = (1.0, 0.6, 0.15)
OMEGA = 0.6
SHIFT = 0.5
RIDGE = 0.1
HALO = SWEEPS
GROUP = 8
BATCH = 13
BATCH_2 = 2
ROWS = True
MESH = pl.DeviceIdType.MESH
F32 = jnp.float32
BF16 = jnp.bfloat16


def smear_z(x):
    axis = x.ndim - 1
    depth = x.shape[axis]
    lane = lax.broadcasted_iota(jnp.int32, x.shape, axis)
    below = jnp.where(lane == 0, 0.0, pltpu.roll(x, 1, axis))
    above = jnp.where(lane == depth - 1, 0.0, pltpu.roll(x, depth - 1, axis))
    return x + ANISOTROPY[2] * (below + above)


def smear_xy(ref, row, col, pick):
    return pick(ref, row, col) + ANISOTROPY[0] * (pick(ref, row - 1, col) + pick(ref, row + 1, col))


def smear_row(ref, row, first, last, pick):
    across = {col: smear_xy(ref, row, col, pick) for col in range(first - 1, last + 1)}
    return [
        smear_z(across[col] + ANISOTROPY[1] * (across[col - 1] + across[col + 1]))
        for col in range(first, last)
    ]


def span(move, size):
    if move == 0:
        return pl.ds(0, size), pl.ds(HALO, size)
    if move > 0:
        return pl.ds(size - HALO, HALO), pl.ds(0, HALO)
    return pl.ds(0, HALO), pl.ds(size + HALO, HALO)


def hole(move, size):
    if move == 0:
        return pl.ds(HALO, size)
    return pl.ds(size + HALO, HALO) if move > 0 else pl.ds(0, HALO)


def rim(move, size):
    if move == 0:
        return pl.ds(1, size)
    return pl.ds(size + 1, 1) if move > 0 else pl.ds(0, 1)


def smooth_kernel(
    nx, ny, nv, raw_ref, k_ref, c_ref, out_ref, knots_ref, spots_ref,
    one, two, gain, wide_k, wide_c, ksend, krecv, csend, crecv, vsend, vrecv,
    fsend, frecv, hsend, hrecv, v_ref, turn,
):
    size_x, size_y, vecs, depth = v_ref.shape
    wide_x, wide_y = size_x + 2 * HALO, size_y + 2 * HALO
    gx, gy, gv = lax.axis_index("gx"), lax.axis_index("gy"), lax.axis_index("vert")
    moves = [(mx, my) for mx in (-1, 0, 1) for my in (-1, 0, 1) if (mx, my) != (0, 0)]

    def inside(mx, my):
        ok_x = jnp.logical_and(gx + mx >= 0, gx + mx < nx)
        ok_y = jnp.logical_and(gy + my >= 0, gy + my < ny)
        return jnp.logical_and(ok_x, ok_y)

    turns = [
        pltpu.make_async_copy(raw_ref.at[vec], v_ref.at[:, :, vec], turn.at[vec])
        for vec in range(vecs)
    ]
    for copy in turns:
        copy.start()

    barrier = pltpu.get_barrier_semaphore()
    total = jnp.int32(nv - 1)
    for mx, my in moves:
        here = inside(mx, my)

        @pl.when(here)
        def _():
            pl.semaphore_signal(
                barrier, inc=1, device_id=(gx + mx, gy + my, gv), device_id_type=MESH
            )

        total = total + here.astype(jnp.int32)
    for step in range(1, nv):
        pl.semaphore_signal(
            barrier, inc=1, device_id=(gx, gy, lax.rem(gv + step, nv)), device_id_type=MESH
        )
    pl.semaphore_wait(barrier, total)

    kinds = (
        (k_ref, wide_k, ksend, krecv), (v_ref, one, vsend, vrecv), (c_ref, wide_c, csend, crecv),
    )

    def departure(kind, no):
        mx, my = moves[no]
        source, target, send, recv = kinds[kind]
        from_x, to_x = span(mx, size_x)
        from_y, to_y = span(my, size_y)
        return pltpu.make_async_remote_copy(
            src_ref=source.at[from_x, from_y], dst_ref=target.at[to_x, to_y],
            send_sem=send.at[no], recv_sem=recv.at[no],
            device_id=(gx + mx, gy + my, gv), device_id_type=MESH,
        )

    def arrival(kind, no):
        mx, my = moves[no]
        other = moves.index((-mx, -my))
        _, target, send, recv = kinds[kind]
        place = target.at[hole(mx, size_x), hole(my, size_y)]
        return pltpu.make_async_remote_copy(
            src_ref=place, dst_ref=place, send_sem=send.at[other], recv_sem=recv.at[other],
            device_id=(gx + mx, gy + my, gv), device_id_type=MESH,
        )

    for no, (mx, my) in enumerate(moves):

        @pl.when(inside(mx, my))
        def _():
            departure(0, no).start()

        @pl.when(jnp.logical_not(inside(mx, my)))
        def _():
            at_x, at_y = hole(mx, size_x), hole(my, size_y)
            for source, target, _, _ in kinds:
                target[at_x, at_y] = jnp.zeros(
                    (at_x.size, at_y.size) + source.shape[2:], source.dtype
                )
            rim_x, rim_y = rim(mx, size_x), rim(my, size_y)
            out_ref[:, rim_x, rim_y] = jnp.zeros((nv, rim_x.size, rim_y.size, vecs, depth), F32)

    for copy in turns:
        copy.wait()
    for kind in (1, 2):
        for no, (mx, my) in enumerate(moves):

            @pl.when(inside(mx, my))
            def _():
                departure(kind, no).start()

    for source, target, _, _ in kinds:
        target[pl.ds(HALO, size_x), pl.ds(HALO, size_y)] = source[...]

    for no, (mx, my) in enumerate(moves):

        @pl.when(inside(mx, my))
        def _():
            arrival(0, no).wait_recv()

    def pick_k(ref, row, col):
        return ref[row, col, 0:1, :]

    def pick_u(ref, row, col):
        return ref[row, col]

    def gains(row, carry):
        around = smear_row(wide_k, row, 1, wide_y - 1, pick_k)
        for col in range(1, wide_y - 1):
            mid = pick_k(wide_k, row, col)
            below = around[col - 1] - (1.0 - SHIFT) * mid
            alive = mid > 0.0
            value = jnp.where(alive, OMEGA * mid / jnp.where(alive, below, 1.0), 0.0)
            gain[row, col] = jnp.broadcast_to(value, (vecs, depth))
        return carry

    lax.fori_loop(1, wide_x - 1, gains, 0, unroll=2)

    for no, (mx, my) in enumerate(moves):

        @pl.when(inside(mx, my))
        def _():
            arrival(1, no).wait_recv()

    def scale(row, carry):
        for col in range(wide_y):
            one[row, col] = one[row, col] * jnp.broadcast_to(pick_k(wide_k, row, col), (vecs, depth))
        return carry

    lax.fori_loop(0, wide_x, scale, 0, unroll=2)

    def relaxed(ref, row, first, last):
        around = smear_row(ref, row, first, last, pick_u)
        result = []
        for col in range(first, last):
            factor = gain[row, col]
            result.append((1.0 - OMEGA - factor) * ref[row, col] + factor * around[col - first])
        return result

    source, target = one, two
    for sweep in range(1, SWEEPS):

        def step(row, carry, source=source, target=target, sweep=sweep):
            for no, value in enumerate(relaxed(source, row, sweep, wide_y - sweep)):
                target[row, sweep + no] = value
            return carry

        lax.fori_loop(sweep, wide_x - sweep, step, 0, unroll=2)
        source, target = target, source

    def last_sweep(row, carry):
        for no, value in enumerate(relaxed(source, row, SWEEPS, wide_y - SWEEPS)):
            out_ref[gv, row - SWEEPS + 1, no + 1] = value
        return carry

    lax.fori_loop(SWEEPS, wide_x - SWEEPS, last_sweep, 0, unroll=2)

    pieces = (
        (pl.ds(1, 1), pl.ds(1, size_y)),
        (pl.ds(size_x, 1), pl.ds(1, size_y)),
        (pl.ds(2, size_x - 2), pl.ds(1, 1)),
        (pl.ds(2, size_x - 2), pl.ds(size_y, 1)),
        (pl.ds(2, size_x - 2), pl.ds(2, size_y - 2)),
    )

    def piece_copy(no, step, half):
        place = out_ref.at[(half,) + pieces[no]]
        return pltpu.make_async_remote_copy(
            src_ref=place, dst_ref=place,
            send_sem=fsend.at[step - 1, no], recv_sem=frecv.at[step - 1, no],
            device_id=(gx, gy, lax.rem(gv + step, nv)), device_id_type=MESH,
        )

    def edge(move, size):
        if move == 0:
            return pl.ds(1, size), pl.ds(1, size)
        if move > 0:
            return pl.ds(size, 1), pl.ds(0, 1)
        return pl.ds(1, 1), pl.ds(size + 1, 1)

    def rim_departure(step, half, no):
        mx, my = moves[no]
        from_x, to_x = edge(mx, size_x)
        from_y, to_y = edge(my, size_y)
        return pltpu.make_async_remote_copy(
            src_ref=out_ref.at[half, from_x, from_y], dst_ref=out_ref.at[half, to_x, to_y],
            send_sem=hsend.at[step, no], recv_sem=hrecv.at[step, no],
            device_id=(gx + mx, gy + my, gv), device_id_type=MESH,
        )

    def rim_arrival(step, half, no):
        mx, my = moves[no]
        other = moves.index((-mx, -my))
        place = out_ref.at[half, edge(-mx, size_x)[1], edge(-my, size_y)[1]]
        return pltpu.make_async_remote_copy(
            src_ref=place, dst_ref=place,
            send_sem=hsend.at[step, other], recv_sem=hrecv.at[step, other],
            device_id=(gx + mx, gy + my, gv), device_id_type=MESH,
        )

    for no in range(len(pieces)):
        for step in range(1, nv):
            piece_copy(no, step, gv).start()
    for step in range(nv):
        half = lax.rem(gv - step + nv, nv)
        if step > 0:
            for no in range(len(pieces) - 1):
                piece_copy(no, step, half).wait_recv()
        for no, (mx, my) in enumerate(moves):

            @pl.when(inside(mx, my))
            def _():
                rim_departure(step, half, no).start()

    for no, (mx, my) in enumerate(moves):

        @pl.when(inside(mx, my))
        def _():
            arrival(2, no).wait_recv()

    rim_x, rim_y = pl.ds(HALO - 1, size_x + 2), pl.ds(HALO - 1, size_y + 2)
    knots_ref[...] = wide_k[rim_x, rim_y]
    spots_ref[...] = wide_c[rim_x, rim_y]

    for step in range(1, nv):
        piece_copy(len(pieces) - 1, step, lax.rem(gv - step + nv, nv)).wait_recv()
        for no in range(len(pieces)):
            piece_copy(no, step, gv).wait_send()
    for no, (mx, my) in enumerate(moves):

        @pl.when(inside(mx, my))
        def _():
            for kind in range(3):
                departure(kind, no).wait_send()
            for step in range(nv):
                half = lax.rem(gv - step + nv, nv)
                rim_arrival(step, half, no).wait_recv()
                rim_departure(step, half, no).wait_send()


def split(x):
    high = x.astype(BF16)
    return high, (x - high.astype(F32)).astype(BF16)


NT = (((1,), (1,)), ((), ()))
NN = (((1,), (0,)), ((), ()))


def dot(a, b, dims):
    return lax.dot_general(a, b, dims, preferred_element_type=F32)


def dot3(a, b, dims):
    return dot(a[0], b[0], dims) + dot(a[0], b[1], dims) + dot(a[1], b[0], dims)


def coarse_kernel(
    size_x, size_y, slots, f_ref, k_ref, c_ref, interp_ref, coarse_ref,
    hot, right_h, right_l, gram_s, lh, ll, rh, rl, ch,
):
    nv, cols, vecs, depth = f_ref.shape
    wide_y = size_y + 2
    rows = GROUP * slots
    members = GROUP * nv * vecs
    count = gram_s.shape[0]
    padded = -(-wide_y // GROUP) * GROUP
    band = size_y * slots

    def lanes(shape):
        return lax.broadcasted_iota(jnp.int32, shape, len(shape) - 1)

    def subs(shape):
        return lax.broadcasted_iota(jnp.int32, shape, len(shape) - 2)

    same = subs((rows, members)) // slots == lanes((rows, members)) // (nv * vecs)
    same_slots = subs((rows, rows)) // slots == lanes((rows, rows)) // slots
    own_lane = subs((rows, slots)) % slots == lanes((rows, slots))
    ones = jnp.ones((slots, depth), BF16)

    def start_of(no):
        return jnp.minimum(no * GROUP, cols - GROUP)

    def gather(batch):
        fields, spreads = [], []
        for no in batch:
            start = min(no * GROUP, cols - GROUP)
            knots = k_ref[pl.ds(start, GROUP)]
            alive = knots > 0.0
            inverse = jnp.where(alive, 1.0 / jnp.where(alive, knots, 1.0), 0.0)
            field = jnp.concatenate(
                [f_ref[half, pl.ds(start, GROUP)] * inverse for half in range(nv)], axis=1
            ).reshape(members, depth)
            fields.append(split(field))
            spots = jnp.broadcast_to(
                c_ref[pl.ds(start, GROUP)].astype(F32), (GROUP, slots, slots)
            ).reshape(rows, slots)
            spreads.append(dot(jnp.where(own_lane, spots, 0.0).astype(BF16), ones, NN))
        pairs = []
        for no, spread, (high, low) in zip(batch, spreads, fields):
            onehot = jnp.where(spread == lanes((rows, depth)).astype(F32), 1.0, 0.0).astype(BF16)
            hot[no] = onehot
            pairs.append(dot(onehot, high, NT) + dot(onehot, low, NT))
        pairs = [split(jnp.where(same, cvals, 0.0)) for cvals in pairs]
        grams = [dot3(pair, pair, NT) for pair in pairs]
        rights = [dot3(pair, field, NN) for pair, field in zip(pairs, fields)]
        for no, gram, right in zip(batch, grams, rights):
            gram_s[no] = jnp.sum(gram.reshape(GROUP, slots, rows), axis=0)
            high, low = split(right)
            right_h[no] = high
            right_l[no] = low

    for first in range(0, count, BATCH):
        gather(range(first, min(first + BATCH, count)))

    shape = (count, slots, rows)
    lane = lanes(shape) % slots
    sub = subs(shape)
    system = gram_s[...]
    diagonal = jnp.sum(jnp.where(lane == sub, system, 0.0), axis=1)
    block = jnp.where(same_slots, 1.0, 0.0).astype(BF16)
    first = diagonal.astype(BF16)
    rest = diagonal - first.astype(F32)
    second = rest.astype(BF16)
    third = (rest - second.astype(F32)).astype(BF16)
    trace = dot(first, block, NN) + dot(second, block, NN) + dot(third, block, NN)
    ridge = RIDGE * trace / slots + 1e-06
    system = system + jnp.where(lane == sub, ridge[:, None, :], 0.0)
    flat = (count * slots, rows)
    base = lanes(flat) // slots * slots
    for pivot in range(slots):
        column = jnp.take_along_axis(
            system.reshape(flat), base + pivot, axis=1, mode="promise_in_bounds"
        ).reshape(shape)
        line = system[:, pivot : pivot + 1, :]
        here = lane[:, 0:1, :] == pivot
        line = jnp.where(here, 1.0, line) / column[:, pivot : pivot + 1, :]
        system = jnp.where(
            sub == pivot, line, jnp.where(lane == pivot, 0.0, system) - column * line
        )
    gram_s[...] = system

    def weigh(batch):
        inverses = [
            split(
                jnp.where(
                    same_slots,
                    jnp.broadcast_to(gram_s[no][None], (GROUP, slots, rows)).reshape(rows, rows),
                    0.0,
                )
            )
            for no in batch
        ]
        solved = [
            dot3(inverse, (right_h[no], right_l[no]), NN) for no, inverse in zip(batch, inverses)
        ]
        for no, weights in zip(batch, solved):
            here = pl.ds(min(no * GROUP, cols - GROUP), GROUP)
            onehot = hot[no].astype(F32).reshape(GROUP, slots, depth)
            crow = jnp.sum(onehot, axis=1, keepdims=True)
            value = weights.reshape(GROUP, slots, depth) * (1.0 - crow) + onehot
            ch[here] = value
            left = value * k_ref[here]
            high, low = split(left)
            lh[here] = high
            ll[here] = low
            high, low = split(smear_z(left.reshape(rows, depth)))
            rh[here] = high.reshape(GROUP, slots, depth)
            rl[here] = low.reshape(GROUP, slots, depth)

    for first in range(0, count, BATCH_2):
        weigh(range(first, min(first + BATCH_2, count)))

    half = GROUP * slots
    groups = slots * slots // half
    tall = (GROUP, half)
    pick_row = lanes(tall) // slots
    out_row = subs(tall)

    def merge(tiles):
        hop = GROUP // 2
        while hop >= 1:
            up = out_row // hop % 2 == 1
            straight = up == (pick_row // hop % 2 == 1)
            merged = []
            for no in range(hop):
                one, two = tiles[no], tiles[no + hop]
                same_place = jnp.where(up, two, one)
                moved = jnp.where(up, one, two)
                down = pltpu.roll(moved, hop, 0)
                if 2 * hop != GROUP:
                    down = jnp.where(up, down, pltpu.roll(moved, GROUP - hop, 0))
                merged.append(jnp.where(straight, same_place, down))
            tiles = merged
            hop //= 2
        return tiles[0]

    block_lane = lanes((slots, half)) % slots

    def galerkin(row, carry):
        at = (row + 1) * wide_y
        mine = pl.ds(at + 1, size_y)
        own = ch[mine]
        interp_ref[row] = own
        across = k_ref[pl.ds(at, wide_y)] + ANISOTROPY[0] * (
            k_ref[pl.ds(at - wide_y, wide_y)] + k_ref[pl.ds(at + wide_y, wide_y)]
        )
        along = across[1 : size_y + 1] + ANISOTROPY[1] * (across[0:size_y] + across[2:])
        whole = smear_z(along.reshape(size_y, depth)).reshape(size_y, 1, depth)
        left = (lh[mine].reshape(band, depth), ll[mine].reshape(band, depth))
        right = rh[mine].astype(F32) + rl[mine].astype(F32)
        centre = right - own * (whole + SHIFT * k_ref[mine])
        middle = dot3(left, split(centre.reshape(band, depth)), NT)
        for move_x in (-1, 0, 1):
            there = pl.ds(at + move_x * wide_y, padded)
            other = (
                rh[there].reshape(padded * slots, depth),
                rl[there].reshape(padded * slots, depth),
            )
            product = dot3(left, other, NT)
            for move_y in (-1, 0, 1):
                weight = 1.0
                if move_x != 0:
                    weight = weight * ANISOTROPY[0]
                if move_y != 0:
                    weight = weight * ANISOTROPY[1]
                order = 3 * (move_x + 1) + move_y + 1
                for chunk in range(0, size_y, GROUP):
                    spread = []
                    for col in range(chunk, chunk + GROUP):
                        central = move_x == 0 and move_y == 0
                        origin = middle if central else product
                        place = col if central else col + 1 + move_y
                        first_lane = place // GROUP * half
                        values = origin[
                            col * slots : (col + 1) * slots, first_lane : first_lane + half
                        ]
                        spread.append(
                            jnp.take_along_axis(
                                values, block_lane + place % GROUP * slots, axis=1,
                                mode="promise_in_bounds",
                            )
                        )
                    parts = [
                        merge([tile[g * GROUP : (g + 1) * GROUP] for tile in spread])
                        for g in range(groups)
                    ]
                    coarse_ref[row, order, chunk : chunk + GROUP, :] = -weight * jnp.concatenate(
                        parts, axis=1
                    )
        return carry

    lax.fori_loop(0, size_x, galerkin, 0, unroll=ROWS)


def body(nx, ny, nv, vectors, conductivity, c_points):
    vecs, size_x, size_y, depth = vectors.shape
    slots = c_points.shape[-1]
    wide_x, wide_y = size_x + 2 * HALO, size_y + 2 * HALO
    cols = (size_x + 2) * (size_y + 2)
    vmem = pl.BlockSpec(memory_space=pltpu.VMEM)
    dma = pltpu.SemaphoreType.DMA
    field, knots, spots = pl.pallas_call(
        functools.partial(smooth_kernel, nx, ny, nv),
        out_shape=(
            jax.ShapeDtypeStruct((nv, size_x + 2, size_y + 2, vecs, depth), F32),
            jax.ShapeDtypeStruct((size_x + 2, size_y + 2, 1, depth), F32),
            jax.ShapeDtypeStruct((size_x + 2, size_y + 2, 1, slots), jnp.int32),
        ),
        in_specs=[pl.BlockSpec(memory_space=pl.ANY), vmem, vmem],
        out_specs=(vmem,) * 3,
        scratch_shapes=[
            pltpu.VMEM((wide_x, wide_y, vecs, depth), F32),
            pltpu.VMEM((wide_x, wide_y, vecs, depth), F32),
            pltpu.VMEM((wide_x, wide_y, vecs, depth), F32),
            pltpu.VMEM((wide_x, wide_y, 1, depth), F32),
            pltpu.VMEM((wide_x, wide_y, 1, slots), jnp.int32),
            dma((8,)), dma((8,)), dma((8,)), dma((8,)), dma((8,)), dma((8,)),
            dma((nv, 5)), dma((nv, 5)), dma((nv, 8)), dma((nv, 8)),
            pltpu.VMEM((size_x, size_y, vecs, depth), F32), dma((vecs,)),
        ],
        compiler_params=pltpu.CompilerParams(collective_id=0, has_side_effects=True),
        name="smooth",
    )(vectors, conductivity[:, :, None, :], c_points[:, :, None, :])
    count = -(-cols // GROUP)
    rows = GROUP * slots
    more = cols + 2 * GROUP
    interp, coarse = pl.pallas_call(
        functools.partial(coarse_kernel, size_x, size_y, slots),
        out_shape=(
            jax.ShapeDtypeStruct((size_x, size_y, slots, depth), F32),
            jax.ShapeDtypeStruct((size_x, 9, size_y, slots * slots), F32),
        ),
        in_specs=[vmem] * 3,
        out_specs=(vmem, vmem),
        scratch_shapes=[
            pltpu.VMEM((count, rows, depth), BF16),
            pltpu.VMEM((count, rows, depth), BF16),
            pltpu.VMEM((count, rows, depth), BF16),
            pltpu.VMEM((count, slots, rows), F32),
            pltpu.VMEM((more, slots, depth), BF16),
            pltpu.VMEM((more, slots, depth), BF16),
            pltpu.VMEM((more, slots, depth), BF16),
            pltpu.VMEM((more, slots, depth), BF16),
            pltpu.VMEM((more, slots, depth), F32),
        ],
        name="coarse",
    )(
        field.reshape(nv, cols, vecs, depth),
        knots.reshape(cols, 1, depth),
        spots.reshape(cols, 1, slots),
    )
    return interp, jnp.transpose(coarse, (0, 2, 1, 3))


def solution(mesh):
    placed = (P("vert", "gx", "gy", None), P("gx", "gy", None), P("gx", "gy", None))
    return jax.shard_map(
        functools.partial(body, mesh.shape["gx"], mesh.shape["gy"], mesh.shape["vert"]),
        mesh=mesh,
        in_specs=placed,
        out_specs=(P("gx", "gy", None, None), P("gx", "gy", None, None)),
        check_vma=False,
    )
```

```python
import functools

import jax
import jax.numpy as jnp
from jax import lax
from jax.experimental import pallas as pl
from jax.experimental.pallas import tpu as pltpu
from jax.sharding import PartitionSpec as P

SWEEPS = 3
ANISOTROPY = (1.0, 0.6, 0.15)
OMEGA = 0.6
SHIFT = 0.5
RIDGE = 0.1
HALO = SWEEPS
GROUP = 8
BATCH = 13
BATCH_2 = 2
ROWS = True
MESH = pl.DeviceIdType.MESH
F32 = jnp.float32
BF16 = jnp.bfloat16


def smear_z(x):
    axis = x.ndim - 1
    depth = x.shape[axis]
    lane = lax.broadcasted_iota(jnp.int32, x.shape, axis)
    below = jnp.where(lane == 0, 0.0, pltpu.roll(x, 1, axis))
    above = jnp.where(lane == depth - 1, 0.0, pltpu.roll(x, depth - 1, axis))
    return x + ANISOTROPY[2] * (below + above)


def smear_xy(ref, row, col, pick):
    return pick(ref, row, col) + ANISOTROPY[0] * (pick(ref, row - 1, col) + pick(ref, row + 1, col))


def smear_row(ref, row, first, last, pick):
    across = {col: smear_xy(ref, row, col, pick) for col in range(first - 1, last + 1)}
    return [
        smear_z(across[col] + ANISOTROPY[1] * (across[col - 1] + across[col + 1]))
        for col in range(first, last)
    ]


def span(move, size, deep):
    if move == 0:
        return pl.ds(0, size), pl.ds(HALO, size)
    if move > 0:
        return pl.ds(size - deep, deep), pl.ds(HALO - deep, deep)
    return pl.ds(0, deep), pl.ds(size + HALO, deep)


def hole(move, size, deep=HALO):
    if move == 0:
        return pl.ds(HALO, size)
    return pl.ds(size + HALO, deep) if move > 0 else pl.ds(HALO - deep, deep)


def rim(move, size):
    if move == 0:
        return pl.ds(1, size)
    return pl.ds(size + 1, 1) if move > 0 else pl.ds(0, 1)


def smooth_kernel(
    nx, ny, nv, raw_ref, k_ref, c_ref, out_ref, knots_ref, spots_ref,
    one, two, gain, wide_k, wide_c, ksend, krecv, csend, crecv, vsend, vrecv,
    fsend, frecv, hsend, hrecv, v_ref, turn,
):
    size_x, size_y, vecs, depth = v_ref.shape
    wide_x, wide_y = size_x + 2 * HALO, size_y + 2 * HALO
    gx, gy, gv = lax.axis_index("gx"), lax.axis_index("gy"), lax.axis_index("vert")
    moves = [(mx, my) for mx in (-1, 0, 1) for my in (-1, 0, 1) if (mx, my) != (0, 0)]

    def inside(mx, my):
        ok_x = jnp.logical_and(gx + mx >= 0, gx + mx < nx)
        ok_y = jnp.logical_and(gy + my >= 0, gy + my < ny)
        return jnp.logical_and(ok_x, ok_y)

    turns = [
        pltpu.make_async_copy(raw_ref.at[vec], v_ref.at[:, :, vec], turn.at[vec])
        for vec in range(vecs)
    ]
    for copy in turns:
        copy.start()

    barrier = pltpu.get_barrier_semaphore()
    total = jnp.int32(nv - 1)
    for mx, my in moves:
        here = inside(mx, my)

        @pl.when(here)
        def _():
            pl.semaphore_signal(
                barrier, inc=1, device_id=(gx + mx, gy + my, gv), device_id_type=MESH
            )

        total = total + here.astype(jnp.int32)
    for step in range(1, nv):
        pl.semaphore_signal(
            barrier, inc=1, device_id=(gx, gy, lax.rem(gv + step, nv)), device_id_type=MESH
        )
    pl.semaphore_wait(barrier, total)

    kinds = (
        (k_ref, wide_k, ksend, krecv), (v_ref, one, vsend, vrecv), (c_ref, wide_c, csend, crecv),
    )

    depths = (HALO, HALO, 1)

    def departure(kind, no):
        mx, my = moves[no]
        source, target, send, recv = kinds[kind]
        from_x, to_x = span(mx, size_x, depths[kind])
        from_y, to_y = span(my, size_y, depths[kind])
        return pltpu.make_async_remote_copy(
            src_ref=source.at[from_x, from_y], dst_ref=target.at[to_x, to_y],
            send_sem=send.at[no], recv_sem=recv.at[no],
            device_id=(gx + mx, gy + my, gv), device_id_type=MESH,
        )

    def arrival(kind, no):
        mx, my = moves[no]
        other = moves.index((-mx, -my))
        _, target, send, recv = kinds[kind]
        place = target.at[hole(mx, size_x, depths[kind]), hole(my, size_y, depths[kind])]
        return pltpu.make_async_remote_copy(
            src_ref=place, dst_ref=place, send_sem=send.at[other], recv_sem=recv.at[other],
            device_id=(gx + mx, gy + my, gv), device_id_type=MESH,
        )

    for no, (mx, my) in enumerate(moves):

        @pl.when(inside(mx, my))
        def _():
            departure(0, no).start()

        @pl.when(jnp.logical_not(inside(mx, my)))
        def _():
            at_x, at_y = hole(mx, size_x), hole(my, size_y)
            for source, target, _, _ in kinds:
                target[at_x, at_y] = jnp.zeros(
                    (at_x.size, at_y.size) + source.shape[2:], source.dtype
                )
            rim_x, rim_y = rim(mx, size_x), rim(my, size_y)
            out_ref[:, rim_x, rim_y] = jnp.zeros((nv, rim_x.size, rim_y.size, vecs, depth), F32)

    for copy in turns:
        copy.wait()
    for kind in (1, 2):
        for no, (mx, my) in enumerate(moves):

            @pl.when(inside(mx, my))
            def _():
                departure(kind, no).start()

    for source, target, _, _ in kinds:
        target[pl.ds(HALO, size_x), pl.ds(HALO, size_y)] = source[...]

    for no, (mx, my) in enumerate(moves):

        @pl.when(inside(mx, my))
        def _():
            arrival(0, no).wait_recv()

    def pick_k(ref, row, col):
        return ref[row, col, 0:1, :]

    def pick_u(ref, row, col):
        return ref[row, col]

    def gains(row, carry):
        around = smear_row(wide_k, row, 1, wide_y - 1, pick_k)
        for col in range(1, wide_y - 1):
            mid = pick_k(wide_k, row, col)
            below = around[col - 1] - (1.0 - SHIFT) * mid
            alive = mid > 0.0
            value = jnp.where(alive, OMEGA * mid / jnp.where(alive, below, 1.0), 0.0)
            gain[row, col] = jnp.broadcast_to(value, (vecs, depth))
        return carry

    lax.fori_loop(1, wide_x - 1, gains, 0, unroll=2)

    for no, (mx, my) in enumerate(moves):

        @pl.when(inside(mx, my))
        def _():
            arrival(1, no).wait_recv()

    def scale(row, carry):
        for col in range(wide_y):
            one[row, col] = one[row, col] * jnp.broadcast_to(pick_k(wide_k, row, col), (vecs, depth))
        return carry

    lax.fori_loop(0, wide_x, scale, 0, unroll=2)

    def relaxed(ref, row, first, last):
        around = smear_row(ref, row, first, last, pick_u)
        result = []
        for col in range(first, last):
            factor = gain[row, col]
            result.append((1.0 - OMEGA - factor) * ref[row, col] + factor * around[col - first])
        return result

    source, target = one, two
    for sweep in range(1, SWEEPS):

        def step(row, carry, source=source, target=target, sweep=sweep):
            for no, value in enumerate(relaxed(source, row, sweep, wide_y - sweep)):
                target[row, sweep + no] = value
            return carry

        lax.fori_loop(sweep, wide_x - sweep, step, 0, unroll=2)
        source, target = target, source

    def last_sweep(row, carry):
        for no, value in enumerate(relaxed(source, row, SWEEPS, wide_y - SWEEPS)):
            out_ref[gv, row - SWEEPS + 1, no + 1] = value
        return carry

    lax.fori_loop(SWEEPS, wide_x - SWEEPS, last_sweep, 0, unroll=2)

    pieces = (
        (pl.ds(1, 1), pl.ds(1, size_y)),
        (pl.ds(size_x, 1), pl.ds(1, size_y)),
        (pl.ds(2, size_x - 2), pl.ds(1, 1)),
        (pl.ds(2, size_x - 2), pl.ds(size_y, 1)),
        (pl.ds(2, size_x - 2), pl.ds(2, size_y - 2)),
    )

    def piece_copy(no, step, half):
        place = out_ref.at[(half,) + pieces[no]]
        return pltpu.make_async_remote_copy(
            src_ref=place, dst_ref=place,
            send_sem=fsend.at[step - 1, no], recv_sem=frecv.at[step - 1, no],
            device_id=(gx, gy, lax.rem(gv + step, nv)), device_id_type=MESH,
        )

    def edge(move, size):
        if move == 0:
            return pl.ds(1, size), pl.ds(1, size)
        if move > 0:
            return pl.ds(size, 1), pl.ds(0, 1)
        return pl.ds(1, 1), pl.ds(size + 1, 1)

    def rim_departure(step, half, no):
        mx, my = moves[no]
        from_x, to_x = edge(mx, size_x)
        from_y, to_y = edge(my, size_y)
        return pltpu.make_async_remote_copy(
            src_ref=out_ref.at[half, from_x, from_y], dst_ref=out_ref.at[half, to_x, to_y],
            send_sem=hsend.at[step, no], recv_sem=hrecv.at[step, no],
            device_id=(gx + mx, gy + my, gv), device_id_type=MESH,
        )

    def rim_arrival(step, half, no):
        mx, my = moves[no]
        other = moves.index((-mx, -my))
        place = out_ref.at[half, edge(-mx, size_x)[1], edge(-my, size_y)[1]]
        return pltpu.make_async_remote_copy(
            src_ref=place, dst_ref=place,
            send_sem=hsend.at[step, other], recv_sem=hrecv.at[step, other],
            device_id=(gx + mx, gy + my, gv), device_id_type=MESH,
        )

    for no in range(len(pieces)):
        for step in range(1, nv):
            piece_copy(no, step, gv).start()
    for step in range(nv):
        half = lax.rem(gv - step + nv, nv)
        if step > 0:
            for no in range(len(pieces) - 1):
                piece_copy(no, step, half).wait_recv()
        for no, (mx, my) in enumerate(moves):

            @pl.when(inside(mx, my))
            def _():
                rim_departure(step, half, no).start()

    for no, (mx, my) in enumerate(moves):

        @pl.when(inside(mx, my))
        def _():
            arrival(2, no).wait_recv()

    rim_x, rim_y = pl.ds(HALO - 1, size_x + 2), pl.ds(HALO - 1, size_y + 2)
    knots_ref[...] = wide_k[rim_x, rim_y]
    spots_ref[...] = wide_c[rim_x, rim_y]

    for step in range(1, nv):
        piece_copy(len(pieces) - 1, step, lax.rem(gv - step + nv, nv)).wait_recv()
        for no in range(len(pieces)):
            piece_copy(no, step, gv).wait_send()
    for no, (mx, my) in enumerate(moves):

        @pl.when(inside(mx, my))
        def _():
            for kind in range(3):
                departure(kind, no).wait_send()
            for step in range(nv):
                half = lax.rem(gv - step + nv, nv)
                rim_arrival(step, half, no).wait_recv()
                rim_departure(step, half, no).wait_send()


def split(x):
    high = x.astype(BF16)
    return high, (x - high.astype(F32)).astype(BF16)


NT = (((1,), (1,)), ((), ()))
NN = (((1,), (0,)), ((), ()))


def dot(a, b, dims):
    return lax.dot_general(a, b, dims, preferred_element_type=F32)


def dot3(a, b, dims):
    return dot(a[0], b[0], dims) + dot(a[0], b[1], dims) + dot(a[1], b[0], dims)


def coarse_kernel(
    size_x, size_y, slots, f_ref, k_ref, c_ref, interp_ref, coarse_ref,
    hot, right_h, right_l, gram_s, lh, ll, rh, rl, ch,
):
    nv, cols, vecs, depth = f_ref.shape
    wide_y = size_y + 2
    rows = GROUP * slots
    members = GROUP * nv * vecs
    count = gram_s.shape[0]
    padded = -(-wide_y // GROUP) * GROUP
    band = size_y * slots

    def lanes(shape):
        return lax.broadcasted_iota(jnp.int32, shape, len(shape) - 1)

    def subs(shape):
        return lax.broadcasted_iota(jnp.int32, shape, len(shape) - 2)

    same = subs((rows, members)) // slots == lanes((rows, members)) // (nv * vecs)
    same_slots = subs((rows, rows)) // slots == lanes((rows, rows)) // slots
    own_lane = subs((rows, slots)) % slots == lanes((rows, slots))
    ones = jnp.ones((slots, depth), BF16)

    def start_of(no):
        return jnp.minimum(no * GROUP, cols - GROUP)

    def gather(batch):
        fields, spreads = [], []
        for no in batch:
            start = min(no * GROUP, cols - GROUP)
            knots = k_ref[pl.ds(start, GROUP)]
            alive = knots > 0.0
            inverse = jnp.where(alive, 1.0 / jnp.where(alive, knots, 1.0), 0.0)
            field = jnp.concatenate(
                [f_ref[half, pl.ds(start, GROUP)] * inverse for half in range(nv)], axis=1
            ).reshape(members, depth)
            fields.append(split(field))
            spots = jnp.broadcast_to(
                c_ref[pl.ds(start, GROUP)].astype(F32), (GROUP, slots, slots)
            ).reshape(rows, slots)
            spreads.append(dot(jnp.where(own_lane, spots, 0.0).astype(BF16), ones, NN))
        pairs = []
        for no, spread, (high, low) in zip(batch, spreads, fields):
            onehot = jnp.where(spread == lanes((rows, depth)).astype(F32), 1.0, 0.0).astype(BF16)
            hot[no] = onehot
            pairs.append(dot(onehot, high, NT) + dot(onehot, low, NT))
        pairs = [split(jnp.where(same, cvals, 0.0)) for cvals in pairs]
        grams = [dot3(pair, pair, NT) for pair in pairs]
        rights = [dot3(pair, field, NN) for pair, field in zip(pairs, fields)]
        for no, gram, right in zip(batch, grams, rights):
            gram_s[no] = jnp.sum(gram.reshape(GROUP, slots, rows), axis=0)
            high, low = split(right)
            right_h[no] = high
            right_l[no] = low

    for first in range(0, count, BATCH):
        gather(range(first, min(first + BATCH, count)))

    shape = (count, slots, rows)
    lane = lanes(shape) % slots
    sub = subs(shape)
    system = gram_s[...]
    diagonal = jnp.sum(jnp.where(lane == sub, system, 0.0), axis=1)
    block = jnp.where(same_slots, 1.0, 0.0).astype(BF16)
    first = diagonal.astype(BF16)
    rest = diagonal - first.astype(F32)
    second = rest.astype(BF16)
    third = (rest - second.astype(F32)).astype(BF16)
    trace = dot(first, block, NN) + dot(second, block, NN) + dot(third, block, NN)
    ridge = RIDGE * trace / slots + 1e-06
    system = system + jnp.where(lane == sub, ridge[:, None, :], 0.0)
    flat = (count * slots, rows)
    base = lanes(flat) // slots * slots
    for pivot in range(slots):
        column = jnp.take_along_axis(
            system.reshape(flat), base + pivot, axis=1, mode="promise_in_bounds"
        ).reshape(shape)
        line = system[:, pivot : pivot + 1, :]
        here = lane[:, 0:1, :] == pivot
        line = jnp.where(here, 1.0, line) / column[:, pivot : pivot + 1, :]
        system = jnp.where(
            sub == pivot, line, jnp.where(lane == pivot, 0.0, system) - column * line
        )
    gram_s[...] = system

    def weigh(batch):
        inverses = [
            split(
                jnp.where(
                    same_slots,
                    jnp.broadcast_to(gram_s[no][None], (GROUP, slots, rows)).reshape(rows, rows),
                    0.0,
                )
            )
            for no in batch
        ]
        solved = [
            dot3(inverse, (right_h[no], right_l[no]), NN) for no, inverse in zip(batch, inverses)
        ]
        for no, weights in zip(batch, solved):
            here = pl.ds(min(no * GROUP, cols - GROUP), GROUP)
            onehot = hot[no].astype(F32).reshape(GROUP, slots, depth)
            crow = jnp.sum(onehot, axis=1, keepdims=True)
            value = weights.reshape(GROUP, slots, depth) * (1.0 - crow) + onehot
            ch[here] = value
            left = value * k_ref[here]
            high, low = split(left)
            lh[here] = high
            ll[here] = low
            high, low = split(smear_z(left.reshape(rows, depth)))
            rh[here] = high.reshape(GROUP, slots, depth)
            rl[here] = low.reshape(GROUP, slots, depth)

    for first in range(0, count, BATCH_2):
        weigh(range(first, min(first + BATCH_2, count)))

    half = GROUP * slots
    groups = slots * slots // half
    tall = (GROUP, half)
    pick_row = lanes(tall) // slots
    out_row = subs(tall)

    def merge(tiles):
        hop = GROUP // 2
        while hop >= 1:
            up = out_row // hop % 2 == 1
            straight = up == (pick_row // hop % 2 == 1)
            merged = []
            for no in range(hop):
                one, two = tiles[no], tiles[no + hop]
                same_place = jnp.where(up, two, one)
                moved = jnp.where(up, one, two)
                down = pltpu.roll(moved, hop, 0)
                if 2 * hop != GROUP:
                    down = jnp.where(up, down, pltpu.roll(moved, GROUP - hop, 0))
                merged.append(jnp.where(straight, same_place, down))
            tiles = merged
            hop //= 2
        return tiles[0]

    block_lane = lanes((slots, half)) % slots

    def galerkin(row, carry):
        at = (row + 1) * wide_y
        mine = pl.ds(at + 1, size_y)
        own = ch[mine]
        interp_ref[row] = own
        across = k_ref[pl.ds(at, wide_y)] + ANISOTROPY[0] * (
            k_ref[pl.ds(at - wide_y, wide_y)] + k_ref[pl.ds(at + wide_y, wide_y)]
        )
        along = across[1 : size_y + 1] + ANISOTROPY[1] * (across[0:size_y] + across[2:])
        whole = smear_z(along.reshape(size_y, depth)).reshape(size_y, 1, depth)
        left = (lh[mine].reshape(band, depth), ll[mine].reshape(band, depth))
        right = rh[mine].astype(F32) + rl[mine].astype(F32)
        centre = right - own * (whole + SHIFT * k_ref[mine])
        middle = dot3(left, split(centre.reshape(band, depth)), NT)
        for move_x in (-1, 0, 1):
            there = pl.ds(at + move_x * wide_y, padded)
            other = (
                rh[there].reshape(padded * slots, depth),
                rl[there].reshape(padded * slots, depth),
            )
            product = dot3(left, other, NT)
            for move_y in (-1, 0, 1):
                weight = 1.0
                if move_x != 0:
                    weight = weight * ANISOTROPY[0]
                if move_y != 0:
                    weight = weight * ANISOTROPY[1]
                order = 3 * (move_x + 1) + move_y + 1
                for chunk in range(0, size_y, GROUP):
                    spread = []
                    for col in range(chunk, chunk + GROUP):
                        central = move_x == 0 and move_y == 0
                        origin = middle if central else product
                        place = col if central else col + 1 + move_y
                        first_lane = place // GROUP * half
                        values = origin[
                            col * slots : (col + 1) * slots, first_lane : first_lane + half
                        ]
                        spread.append(
                            jnp.take_along_axis(
                                values, block_lane + place % GROUP * slots, axis=1,
                                mode="promise_in_bounds",
                            )
                        )
                    parts = [
                        merge([tile[g * GROUP : (g + 1) * GROUP] for tile in spread])
                        for g in range(groups)
                    ]
                    coarse_ref[row, order, chunk : chunk + GROUP, :] = -weight * jnp.concatenate(
                        parts, axis=1
                    )
        return carry

    lax.fori_loop(0, size_x, galerkin, 0, unroll=ROWS)


def body(nx, ny, nv, vectors, conductivity, c_points):
    vecs, size_x, size_y, depth = vectors.shape
    slots = c_points.shape[-1]
    wide_x, wide_y = size_x + 2 * HALO, size_y + 2 * HALO
    cols = (size_x + 2) * (size_y + 2)
    vmem = pl.BlockSpec(memory_space=pltpu.VMEM)
    dma = pltpu.SemaphoreType.DMA
    field, knots, spots = pl.pallas_call(
        functools.partial(smooth_kernel, nx, ny, nv),
        out_shape=(
            jax.ShapeDtypeStruct((nv, size_x + 2, size_y + 2, vecs, depth), F32),
            jax.ShapeDtypeStruct((size_x + 2, size_y + 2, 1, depth), F32),
            jax.ShapeDtypeStruct((size_x + 2, size_y + 2, 1, slots), jnp.int32),
        ),
        in_specs=[pl.BlockSpec(memory_space=pl.ANY), vmem, vmem],
        out_specs=(vmem,) * 3,
        scratch_shapes=[
            pltpu.VMEM((wide_x, wide_y, vecs, depth), F32),
            pltpu.VMEM((wide_x, wide_y, vecs, depth), F32),
            pltpu.VMEM((wide_x, wide_y, vecs, depth), F32),
            pltpu.VMEM((wide_x, wide_y, 1, depth), F32),
            pltpu.VMEM((wide_x, wide_y, 1, slots), jnp.int32),
            dma((8,)), dma((8,)), dma((8,)), dma((8,)), dma((8,)), dma((8,)),
            dma((nv, 5)), dma((nv, 5)), dma((nv, 8)), dma((nv, 8)),
            pltpu.VMEM((size_x, size_y, vecs, depth), F32), dma((vecs,)),
        ],
        compiler_params=pltpu.CompilerParams(collective_id=0, has_side_effects=True),
        name="smooth",
    )(vectors, conductivity[:, :, None, :], c_points[:, :, None, :])
    count = -(-cols // GROUP)
    rows = GROUP * slots
    more = cols + 2 * GROUP
    interp, coarse = pl.pallas_call(
        functools.partial(coarse_kernel, size_x, size_y, slots),
        out_shape=(
            jax.ShapeDtypeStruct((size_x, size_y, slots, depth), F32),
            jax.ShapeDtypeStruct((size_x, 9, size_y, slots * slots), F32),
        ),
        in_specs=[vmem] * 3,
        out_specs=(vmem, vmem),
        scratch_shapes=[
            pltpu.VMEM((count, rows, depth), BF16),
            pltpu.VMEM((count, rows, depth), BF16),
            pltpu.VMEM((count, rows, depth), BF16),
            pltpu.VMEM((count, slots, rows), F32),
            pltpu.VMEM((more, slots, depth), BF16),
            pltpu.VMEM((more, slots, depth), BF16),
            pltpu.VMEM((more, slots, depth), BF16),
            pltpu.VMEM((more, slots, depth), BF16),
            pltpu.VMEM((more, slots, depth), F32),
        ],
        name="coarse",
    )(
        field.reshape(nv, cols, vecs, depth),
        knots.reshape(cols, 1, depth),
        spots.reshape(cols, 1, slots),
    )
    return interp, jnp.transpose(coarse, (0, 2, 1, 3))


def solution(mesh):
    placed = (P("vert", "gx", "gy", None), P("gx", "gy", None), P("gx", "gy", None))
    return jax.shard_map(
        functools.partial(body, mesh.shape["gx"], mesh.shape["gy"], mesh.shape["vert"]),
        mesh=mesh,
        in_specs=placed,
        out_specs=(P("gx", "gy", None, None), P("gx", "gy", None, None)),
        check_vma=False,
    )
```
